128 devices in a mesh: lat: 16 (over x_lo, z, core), lon: 8 (over y, x_hi).
Axes of the slice: x: 4 (x_hi: 2, x_lo: 2; x = x_hi * 2 + x_lo), y: 4, z: 4, core: 2. Of those that a mesh axis runs over, the one named last changes fastest.
Arguments:
- forcing: float32 [16, 2048, 2048], P(None, 'lat', 'lon'), may hold values from -6 to 6
- metric_lon: float32 [2048, 2048], P('lat', 'lon'), may hold values from -0.5 to 0.5
- metric_lat: float32 [2048, 2048], P('lat', 'lon'), may hold values from -0.5 to 0.5
- lon_weights: float32 [2048], P('lon'), may hold values from 0.5 to 2
- eigen_basis: float32 [2048, 2048], replicated, may hold values from -0.125 to 0.125
- lower_mult: float32 [16, 2048, 2048], P('lon', 'lat'), may hold values from -1 to 0
- pivot_inverse: float32 [16, 2048, 2048], P('lon', 'lat'), may hold values from 0 to 2
- upper_coef: float32 [16, 2048, 2048], P('lon', 'lat'), may hold values from -33554432 to 0
Outputs:
- solution: float32 [16, 2048, 2048], P(None, 'lat', 'lon')
The draws below stay inside these ranges and needn't reach their ends.
All inputs are finite; a program needn't handle non-finite values.
Results may differ from the reference program's by a relative error of at most 0.000082.
Values sent between devices are 32-bit elements; how exact they have to be, the bound alone decides.
A program may use at most 128 MiB of HBM per device.

```python
import math
import jax
import jax.numpy as jnp
from jax import lax

NLON = 2048
K = 16
LATITUDE_COUNT = 2048


def latitude_factors(key):
    random_keys = jax.random.split(jax.random.fold_in(key, 11), 5)
    shape = (K, LATITUDE_COUNT, NLON)
    share = 0.5
    sluggish_columns = jax.random.uniform(random_keys[0], (K, 1, NLON)) < share
    baseline_loss = jnp.where(sluggish_columns, 1.0 / LATITUDE_COUNT, 1.0 / 40.0).astype(jnp.float32)
    spike_rows = jax.random.randint(random_keys[1], (3,), 0, LATITUDE_COUNT)
    spike_mask = jnp.any(jnp.arange(LATITUDE_COUNT)[:, None] == spike_rows[None, :], axis=1)[None, :, None]
    spike_scale = jnp.where(spike_mask & sluggish_columns, 0.7, 1.0).astype(jnp.float32)
    low_log = jnp.log(0.5)
    high_log = jnp.log(2.0)
    jagged_downward = jnp.exp(jax.random.uniform(random_keys[2], shape, jnp.float32, low_log, high_log))
    jagged_upward = jnp.exp(jax.random.uniform(random_keys[3], shape, jnp.float32, low_log, high_log))
    scale_draw = jnp.exp(jax.random.uniform(random_keys[4], shape, jnp.float32, low_log, high_log))
    kept_downward = (1.0 - baseline_loss * jagged_downward) * spike_scale
    kept_upward = (1.0 - baseline_loss * jagged_upward) * spike_scale
    pivots = (1.0 - kept_upward) * jnp.sqrt(1.0 - kept_downward * kept_downward) * scale_draw
    return (-kept_downward, pivots, -kept_upward / pivots)


def draw_lower_mult(key, part):
    return latitude_factors(key)[0]


def draw_pivot_inverse(key, part):
    return latitude_factors(key)[1]


def draw_upper_coef(key, part):
    return latitude_factors(key)[2]


def steps_of(key, extent, cuts, least, high):
    gain, own = 1.0, jax.random.fold_in(key, 6)
    for axis_at, blocks in cuts:
        draws = jnp.exp(jax.random.uniform(jax.random.fold_in(own, axis_at), (blocks,), jnp.float32, least / len(cuts), high / len(cuts)))
        gain = gain * jnp.repeat(draws, extent[axis_at] // blocks).reshape([-1 if axis == axis_at else 1 for axis in range(len(extent))])
    return gain


def noise(own_key, dims, scale, bound, cuts=(), dtype=jnp.bfloat16):
    result = scale * jax.random.normal(own_key, dims, jnp.float32)
    if cuts:
        result = result * steps_of(own_key, dims, cuts, -0.22, 0.18)
    return jnp.clip(result, -bound, bound).astype(dtype)


def setup_inputs(seed: int = 0) -> dict:
    key_list = jax.random.split(jax.random.key(seed), 9)
    return {
        "forcing": noise(key_list[0], (K, LATITUDE_COUNT, NLON), 1.0, 6.0, ((1, 16), (2, 8)), jnp.float32),
        "metric_lon": jnp.clip(jax.random.uniform(key_list[1], (LATITUDE_COUNT, NLON), jnp.float32, -0.5, 0.5) * steps_of(key_list[1], (LATITUDE_COUNT, NLON), ((0, 16), (1, 8)), -0.4, 0.0), -0.5, 0.5),
        "metric_lat": jnp.clip(jax.random.uniform(key_list[2], (LATITUDE_COUNT, NLON), jnp.float32, -0.5, 0.5) * steps_of(key_list[2], (LATITUDE_COUNT, NLON), ((0, 16), (1, 8)), -0.4, 0.0), -0.5, 0.5),
        "lon_weights": jnp.clip(jnp.exp(math.log(2.0) - 1.3862944 * jax.random.uniform(key_list[3], (NLON,), jnp.float32) ** steps_of(key_list[3], (NLON,), ((0, 8),), -0.2, 0.2)), 0.5, 2.0),
        "eigen_basis": noise(key_list[4], (NLON, NLON), NLON ** -0.5, 0.125, (), jnp.float32),
        "lower_mult": draw_lower_mult(jax.random.fold_in(key_list[8], 71), 0),
        "pivot_inverse": draw_pivot_inverse(jax.random.fold_in(key_list[8], 71), 0),
        "upper_coef": draw_upper_coef(jax.random.fold_in(key_list[8], 71), 0),
    }


def reference(forcing, metric_lon, metric_lat, lon_weights, eigen_basis, lower_mult, pivot_inverse, upper_coef):
    west_cells = jnp.roll(forcing, 1, axis=2)
    east_cells = jnp.roll(forcing, -1, axis=2)
    padded = jnp.pad(forcing, ((0, 0), (1, 1), (0, 0)))
    source_term = forcing + metric_lon * (west_cells + east_cells) + metric_lat * (padded[:, :-2, :] + padded[:, 2:, :])
    weighted = source_term * lon_weights
    spectral = jnp.einsum("kji,im->kjm", weighted, eigen_basis, precision=lax.Precision.HIGHEST)

    def forward(state, inputs):
        lower_row, spectral_row = inputs
        updated = spectral_row - lower_row * state
        return updated, updated

    start_state = jnp.zeros((spectral.shape[0], spectral.shape[2]), jnp.float32)
    _, sweep = lax.scan(forward, start_state, (jnp.transpose(lower_mult, (1, 0, 2)), jnp.transpose(spectral, (1, 0, 2))))

    def backward(state, inputs):
        pivot_row, upper_row, sweep_row = inputs
        updated = pivot_row * sweep_row - (upper_row * pivot_row) * state
        return updated, updated

    _, modal = lax.scan(backward, start_state, (jnp.transpose(pivot_inverse, (1, 0, 2)), jnp.transpose(upper_coef, (1, 0, 2)), sweep), reverse=True)
    modal = jnp.transpose(modal, (1, 0, 2))
    return jnp.einsum("kjm,im->kji", modal, eigen_basis, precision=lax.Precision.HIGHEST)
```

```python
import functools

import jax
import jax.numpy as jnp
from jax import lax
from jax.experimental import pallas as pl
from jax.experimental.pallas import tpu as pltpu
from jax.sharding import PartitionSpec as P

MESH = pl.DeviceIdType.MESH
F32, BF16 = jnp.float32, jnp.bfloat16
NN = (((1,), (0,)), ((), ()))
NT = (((1,), (1,)), ((), ()))
TILES = 4
STEPS = 16


def split(x):
    high = x.astype(BF16)
    return high, (x - high.astype(F32)).astype(BF16)


def product(lhs_high, lhs_low, rhs_high, rhs_low, dims):
    dot = functools.partial(lax.dot_general, dimension_numbers=dims, preferred_element_type=F32)
    return dot(lhs_high, rhs_high) + dot(lhs_high, rhs_low) + dot(lhs_low, rhs_high)


def segments_combined(scale, shift, forward):
    row = lax.broadcasted_iota(jnp.int32, scale.shape, 0)

    def moved(x, by):
        return pltpu.roll(x, by if forward else 8 - by, 0)

    def inside(by):
        return row >= by if forward else row < 8 - by

    for by in (1, 2, 4):
        keep = inside(by)
        shift = jnp.where(keep, scale * moved(shift, by) + shift, shift)
        scale = jnp.where(keep, scale * moved(scale, by), scale)
    first = inside(1)
    return (
        scale,
        shift,
        jnp.where(first, moved(scale, 1), 1.0),
        jnp.where(first, moved(shift, 1), 0.0),
    )


def kernel(
    forcing_h, mlon_h, mlat_h, wlon_h, basis_h, low_h, pinv_h, up_h, out_h,
    fpad, mlon, mlat, wlon, row_last, row_first, halo_n, halo_s, edge, halo_w, halo_e, halo_t,
    send1, got1, stage, vh, vl, low, pinv, up, pref, qref, wref,
    xh, xl, body, seg_eq, seg_ew, seg_eb, gc, gd, send2,
    l_in, l_v, l_co, l_own, h_s, h_r, s1, r1, c_s, c_r, d_s, d_r, s2, r2,
):
    a, b = lax.axis_index("lat"), lax.axis_index("lon")
    chip, core = lax.div(a, 2), lax.rem(a, 2)
    copy = pltpu.make_async_copy

    inputs = [
        copy(forcing_h, fpad.at[:, pl.ds(8, 128), :], l_in.at[0]),
        copy(mlon_h, mlon, l_in.at[1]),
        copy(mlat_h, mlat, l_in.at[2]),
        copy(wlon_h, wlon, l_in.at[3]),
    ]
    for c in inputs:
        c.start()

    def basis_rows(i, slot):
        rows = pl.multiple_of(i * 128, 128)
        return copy(basis_h.at[pl.ds(rows, 128)], stage.at[slot], l_v.at[slot])

    coefs = [
        copy(src.at[:, :, pl.ds(c * 128, 128)], dst.at[:, c], l_co.at[i, c])
        for i, (src, dst) in enumerate(((low_h, low), (pinv_h, pinv), (up_h, up)))
        for c in range(16)
    ]

    def lon_peer(o):
        return {"lon": lax.rem(b + o, 8)}

    def lat_peer(o):
        return {"lat": lax.rem(chip + o, 8) * 2 + core}

    partner = {"lat": chip * 2 + 1 - core}
    north, south = {"lat": lax.rem(a + 15, 16)}, {"lat": lax.rem(a + 1, 16)}

    barrier = pltpu.get_barrier_semaphore()
    for peer in [lon_peer(o) for o in range(1, 8)] + [lat_peer(o) for o in range(1, 8)] + [north, south]:
        pl.semaphore_signal(barrier, inc=1, device_id=peer, device_id_type=MESH)

    inputs[0].wait()
    for slot in range(4):
        basis_rows(slot, slot).start()
    for c in coefs:
        c.start()
    lane = lax.broadcasted_iota(jnp.int32, (128, 128), 1)
    columns = jnp.zeros((128, 128), F32)
    for k in range(16):
        row_first[k : k + 1, :] = fpad[k, 8:9, :]
        row_last[k : k + 1, :] = fpad[k, 135:136, :]
        columns = jnp.where(lane == k, fpad[k, 8:136, 255:256], columns)
        columns = jnp.where(lane == 16 + k, fpad[k, 8:136, 0:1], columns)
    edge[...] = columns.T[:32]
    pl.semaphore_wait(barrier, 16)

    def remote(src, dst, send, recv, peer):
        return pltpu.make_async_remote_copy(
            src_ref=src, dst_ref=dst, send_sem=send, recv_sem=recv, device_id=peer, device_id_type=MESH
        )

    halos = [
        remote(edge.at[pl.ds(0, 16)], halo_w, h_s.at[0], h_r.at[0], lon_peer(1)),
        remote(edge.at[pl.ds(16, 16)], halo_e, h_s.at[1], h_r.at[1], lon_peer(7)),
        remote(row_last, halo_n, h_s.at[2], h_r.at[2], south),
        remote(row_first, halo_s, h_s.at[3], h_r.at[3], north),
    ]
    for c in halos:
        c.start()
    for c in inputs[1:]:
        c.wait()
    for c in halos:
        c.wait()
    for k in range(16):
        fpad[k, 7:8, :] = jnp.where(a > 0, halo_n[k : k + 1, :], 0.0)
        fpad[k, 136:137, :] = jnp.where(a < 15, halo_s[k : k + 1, :], 0.0)
    halo_t[...] = jnp.concatenate([halo_w[...], halo_e[...], jnp.zeros((96, 128), F32)], axis=0).T

    lane2 = lax.broadcasted_iota(jnp.int32, (32, 256), 1)

    def source(k, store):
        west_edge, east_edge = pltpu.roll(halo_t[...], 128 - k, 1), pltpu.roll(halo_t[...], 111 - k, 1)
        for r in range(4):
            at, rows = 8 + 32 * r, slice(32 * r, 32 * r + 32)
            f = fpad[k, at : at + 32, :]
            we, ee = west_edge[rows], east_edge[rows]
            west = jnp.where(lane2 == 0, jnp.concatenate([we, we], axis=1), pltpu.roll(f, 1, 1))
            east = jnp.where(lane2 == 255, jnp.concatenate([ee, ee], axis=1), pltpu.roll(f, 255, 1))
            up_down = fpad[k, at - 1 : at + 31, :] + fpad[k, at + 1 : at + 33, :]
            term = f + mlon[rows, :] * (west + east) + mlat[rows, :] * up_down
            store(rows, term * wlon[...])

    def to_lon(p, o):
        return remote(send1.at[p, o], got1.at[p, b], s1.at[p, o], r1.at[p, o], lon_peer(o))

    for p in range(2):

        def send_source(o, carry, p=p):
            d = lax.rem(b + o, 8)

            def store(rows, value):
                send1[p, o, rows, :] = value

            source(2 * d + p, store)
            to_lon(p, o).start()
            return carry

        lax.fori_loop(1, 8, send_source, 0)
    for p in range(2):

        def keep(rows, value, p=p):
            got1[p, b, rows, :] = value

        source(2 * b + p, keep)

    def basis_step(t, carry):
        for slot in range(4):
            i = t * 4 + slot
            basis_rows(i, slot).wait()

            def rows_split(r, c, slot=slot, i=i):
                high, lower = split(stage[slot, pl.ds(pl.multiple_of(r * 16, 16), 16), :])
                to = pl.ds(pl.multiple_of(i * 128 + r * 16, 16), 16)
                vh[to, :] = high
                vl[to, :] = lower
                return c

            lax.fori_loop(0, 8, rows_split, 0)

            @pl.when(t < 3)
            def _(i=i, slot=slot):
                basis_rows(i + 4, slot).start()

        return carry

    lax.fori_loop(0, 4, basis_step, 0)

    for c in coefs:
        c.wait()

    def at_step(g):
        return (pl.ds(g, 8, stride=STEPS), slice(None))

    ones, zeros = jnp.ones((8, 128), F32), jnp.zeros((8, 128), F32)

    for p in range(2):

        def coef_block(cb, carry, p=p):
            for t in range(TILES):
                c = cb * TILES + t
                scale = ones
                for g in range(STEPS):
                    scale = -low[(p, c, *at_step(g))] * scale
                    pref[(p, c, *at_step(g))] = scale
                total, _, enter, _ = segments_combined(scale, zeros, True)
                gc[core, chip, pl.ds(p * 48 + c, 1), :] = total[7:8]
                q, w = ones, zeros
                for g in range(STEPS)[::-1]:
                    at = (p, c, *at_step(g))
                    pivot = pinv[at]
                    u = -(up[at] * pivot)
                    up[at] = u
                    w = pivot * (pref[at] * enter) + u * w
                    q = u * q
                    qref[at] = q
                    wref[at] = w
                total_q, total_w, eq, ew = segments_combined(q, w, False)
                gc[core, chip, pl.ds(p * 48 + 16 + c, 1), :] = total_q[0:1]
                gc[core, chip, pl.ds(p * 48 + 32 + c, 1), :] = total_w[0:1]
                seg_eq[p, c] = eq
                seg_ew[p, c] = ew
            return carry

        lax.fori_loop(0, 16 // TILES, coef_block, 0)

    def coef_to(o):
        return remote(gc.at[core, chip], gc.at[core, chip], c_s.at[o], c_r.at[o], lat_peer(o))

    coef_pair = remote(gc.at[core], gc.at[core], c_s.at[0], c_r.at[0], partner)
    for o in range(1, 8):
        coef_to(o).start()

    def first_half(p):
        for o in range(1, 8):
            to_lon(p, o).wait_recv()

        def split_source(s, carry):
            high, lower = split(got1[p, s])
            cols = pl.ds(pl.multiple_of(s * 256, 256), 256)
            xh[:, cols] = high
            xl[:, cols] = lower
            return carry

        lax.fori_loop(0, 8, split_source, 0)

        def transform(n, carry):
            cols = pl.ds(pl.multiple_of(n * 512, 512), 512)
            block = product(xh[...], xl[...], vh[:, cols], vl[:, cols], NN)
            for t in range(4):
                body[p, n * 4 + t] = block[:, t * 128 : t * 128 + 128]
            return carry

        lax.fori_loop(0, 4, transform, 0)

        def solve_block(cb, carry):
            for t in range(TILES):
                c = cb * TILES + t
                x = zeros
                for g in range(STEPS):
                    at = (p, c, *at_step(g))
                    x = body[at] - low[at] * x
                    body[at] = x
                _, total, _, enter = segments_combined(pref[(p, c, *at_step(STEPS - 1))], x, True)
                gd[p, core, chip, pl.ds(c, 1), :] = total[7:8]
                y = zeros
                for g in range(STEPS)[::-1]:
                    at = (p, c, *at_step(g))
                    y = pinv[at] * (body[at] + pref[at] * enter) + up[at] * y
                    body[at] = y
                _, total, _, enter = segments_combined(qref[(p, c, *at_step(0))], y, False)
                gd[p, core, chip, pl.ds(16 + c, 1), :] = total[0:1]
                seg_eb[p, c] = enter
            return carry

        lax.fori_loop(0, 16 // TILES, solve_block, 0)
        for o in range(1, 8):
            data_to(p, o).start()

    def data_to(p, o):
        return remote(gd.at[p, core, chip], gd.at[p, core, chip], d_s.at[p, o], d_r.at[p, o], lat_peer(o))

    def data_pair(p):
        return remote(gd.at[p, core], gd.at[p, core], d_s.at[p, 0], d_r.at[p, 0], partner)

    def back_to(p, o):
        return remote(send2.at[p, o], out_h.at[2 * b + p], s2.at[p, o], r2.at[p, o], lon_peer(o))

    def second_half(p):
        for o in range(1, 8):
            data_to(p, o).wait_recv()
        data_pair(p).start()
        data_pair(p).wait_recv()
        entering, mine, entries = jnp.zeros((16, 128), F32), jnp.zeros((16, 128), F32), []
        for n in range(16):
            entries.append(entering)
            mine = jnp.where(a == n, entering, mine)
            entering = gc[n % 2, n // 2, p * 48 : p * 48 + 16, :] * entering + gd[p, n % 2, n // 2, 0:16, :]
        arriving, coming = jnp.zeros((16, 128), F32), jnp.zeros((16, 128), F32)
        for n in range(16)[::-1]:
            coming = jnp.where(a == n, arriving, coming)
            top = gd[p, n % 2, n // 2, 16:32, :] + gc[n % 2, n // 2, p * 48 + 32 : p * 48 + 48, :] * entries[n]
            arriving = gc[n % 2, n // 2, p * 48 + 16 : p * 48 + 32, :] * arriving + top
        for c in range(16):
            cols = slice(c * 128, c * 128 + 128)
            ent, arr = mine[c : c + 1], coming[c : c + 1]
            late = seg_eq[p, c] * arr + seg_eb[p, c] + seg_ew[p, c] * ent
            for s in range(8):
                rows = slice(s * 16, s * 16 + 16)
                value = body[p, c, rows] + wref[p, c, rows] * ent + qref[p, c, rows] * late[s : s + 1]
                high, lower = split(value)
                xh[rows, cols] = high
                xl[rows, cols] = lower

        def grid_block(o, carry):
            rows = pl.ds(pl.multiple_of(lax.rem(b + o, 8) * 256, 256), 256)
            send2[p, o] = product(xh[...], xl[...], vh[rows, :], vl[rows, :], NT)
            return carry

        def grid_send(o, carry):
            grid_block(o, carry)
            back_to(p, o).start()
            return carry

        lax.fori_loop(1, 8, grid_send, 0)
        grid_block(0, 0)
        own(p).start()

    def own(p):
        return copy(send2.at[p, 0], out_h.at[2 * b + p], l_own.at[p])

    first_half(0)
    for o in range(1, 8):
        coef_to(o).wait_recv()
    coef_pair.start()
    coef_pair.wait_recv()
    second_half(0)
    first_half(1)
    second_half(1)
    for o in range(1, 8):
        coef_to(o).wait_send()
    coef_pair.wait_send()
    for p in range(2):
        for o in range(1, 8):
            to_lon(p, o).wait_send()
            data_to(p, o).wait_send()
            back_to(p, o).wait_send()
        data_pair(p).wait_send()
        own(p).wait()
    for p in range(2):
        for o in range(1, 8):
            back_to(p, o).wait_recv()


def per_device(forcing, metric_lon, metric_lat, lon_weights, eigen_basis, lower_mult, pivot_inverse, upper_coef):
    vmem, dma = pltpu.VMEM, pltpu.SemaphoreType.DMA
    band = (2, 16, 128, 128)
    scratch = [
        vmem((16, 144, 256), F32), vmem((128, 256), F32), vmem((128, 256), F32), vmem((1, 256), F32),
        vmem((16, 256), F32), vmem((16, 256), F32), vmem((16, 256), F32), vmem((16, 256), F32),
        vmem((32, 128), F32), vmem((16, 128), F32), vmem((16, 128), F32), vmem((128, 128), F32),
        vmem((2, 8, 128, 256), F32), vmem((2, 8, 128, 256), F32), vmem((4, 128, 2048), F32),
        vmem((2048, 2048), BF16), vmem((2048, 2048), BF16),
        vmem(band, F32), vmem(band, F32), vmem(band, F32), vmem(band, F32), vmem(band, F32), vmem(band, F32),
        vmem((128, 2048), BF16), vmem((128, 2048), BF16), vmem(band, F32),
        vmem((2, 16, 8, 128), F32), vmem((2, 16, 8, 128), F32), vmem((2, 16, 8, 128), F32),
        vmem((2, 8, 96, 128), F32), vmem((2, 2, 8, 32, 128), F32), vmem((2, 8, 128, 256), F32),
        dma((4,)), dma((4,)), dma((3, 16)), dma((2,)), dma((4,)), dma((4,)), dma((2, 8)), dma((2, 8)),
        dma((8,)), dma((8,)), dma((2, 8)), dma((2, 8)), dma((2, 8)), dma((2, 8)),
    ]
    return pl.pallas_call(
        kernel,
        out_shape=jax.ShapeDtypeStruct((16, 128, 256), F32),
        in_specs=[pl.BlockSpec(memory_space=pl.ANY)] * 8,
        out_specs=pl.BlockSpec(memory_space=pl.ANY),
        scratch_shapes=scratch,
        compiler_params=pltpu.CompilerParams(collective_id=0, has_side_effects=True, vmem_limit_bytes=60 << 20),
    )(
        forcing, metric_lon, metric_lat, lon_weights.reshape(1, 256), eigen_basis,
        lower_mult, pivot_inverse, upper_coef,
    )


def solution(mesh):
    placed = (
        P(None, "lat", "lon"), P("lat", "lon"), P("lat", "lon"), P("lon"), P(),
        P("lon", "lat", None), P("lon", "lat", None), P("lon", "lat", None),
    )
    return jax.shard_map(
        per_device, mesh=mesh, in_specs=placed, out_specs=P(None, "lat", "lon"), check_vma=False
    )
```

```python
import functools

import jax
import jax.numpy as jnp
from jax import lax
from jax.experimental import pallas as pl
from jax.experimental.pallas import tpu as pltpu
from jax.sharding import PartitionSpec as P

MESH = pl.DeviceIdType.MESH
F32, BF16 = jnp.float32, jnp.bfloat16
NN = (((1,), (0,)), ((), ()))
NT = (((1,), (1,)), ((), ()))
TILES = 4
STEPS = 16
ORDER = (1, 3, 5, 7, 2, 4, 6)
FIRST, BACK_FIRST = 64, 96


def split(x):
    high = x.astype(BF16)
    return high, (x - high.astype(F32)).astype(BF16)


def product(pair, rhs_high, rhs_low, dims):
    dot = functools.partial(lax.dot_general, dimension_numbers=dims, preferred_element_type=F32)
    both = dot(pair, rhs_high)
    return both[:128] + both[128:] + dot(pair[:128], rhs_low)


def segments_combined(scale, shift, forward):
    row = lax.broadcasted_iota(jnp.int32, scale.shape, 0)

    def moved(x, by):
        return pltpu.roll(x, by if forward else 8 - by, 0)

    def inside(by):
        return row >= by if forward else row < 8 - by

    for by in (1, 2, 4):
        keep = inside(by)
        shift = jnp.where(keep, scale * moved(shift, by) + shift, shift)
        scale = jnp.where(keep, scale * moved(scale, by), scale)
    first = inside(1)
    return (
        scale,
        shift,
        jnp.where(first, moved(scale, 1), 1.0),
        jnp.where(first, moved(shift, 1), 0.0),
    )


def kernel(
    forcing_h, mlon_h, mlat_h, wlon_h, basis_h, low_h, pinv_h, up_h, out_h,
    fpad, mlon, mlat, wlon, row_last, row_first, halo_n, halo_s, edge, halo_w, halo_e, halo_t,
    send1, got1, stage, vh, vl, low, pinv, up, pref, qref, wref,
    pair, body, seg_eq, seg_ew, seg_eb, gc, gd, send2,
    fix, fixes, fix_t,
    l_in, l_v, l_co, l_own, h_s, h_r, s1, r1, c_s, c_r, d_s, d_r, s2, r2,
    f_s, f_r, late_s, late_r,
):
    a, b = lax.axis_index("lat"), lax.axis_index("lon")
    chip, core = lax.div(a, 2), lax.rem(a, 2)
    copy = pltpu.make_async_copy

    inputs = [
        copy(forcing_h, fpad.at[:, pl.ds(8, 128), :], l_in.at[0]),
        copy(mlon_h, mlon, l_in.at[1]),
        copy(mlat_h, mlat, l_in.at[2]),
        copy(wlon_h, wlon, l_in.at[3]),
    ]
    for c in inputs:
        c.start()

    def basis_rows(i, slot):
        rows = pl.multiple_of(i * 128, 128)
        return copy(basis_h.at[pl.ds(rows, 128)], stage.at[slot], l_v.at[slot])

    coefs = [
        copy(src.at[:, :, pl.ds(c * 128, 128)], dst.at[:, c], l_co.at[i, c])
        for i, (src, dst) in enumerate(((low_h, low), (pinv_h, pinv), (up_h, up)))
        for c in range(16)
    ]

    def lon_peer(o):
        return {"lon": lax.rem(b + o, 8)}

    def lat_peer(o):
        return {"lat": lax.rem(chip + o, 8) * 2 + core}

    partner = {"lat": chip * 2 + 1 - core}
    north, south = {"lat": lax.rem(a + 15, 16)}, {"lat": lax.rem(a + 1, 16)}

    barrier = pltpu.get_barrier_semaphore()
    for peer in [lon_peer(o) for o in range(1, 8)] + [lat_peer(o) for o in range(1, 8)] + [north, south]:
        pl.semaphore_signal(barrier, inc=1, device_id=peer, device_id_type=MESH)

    for c in inputs:
        c.wait()
    for c in coefs:
        c.start()
    for slot in range(4):
        basis_rows(slot, slot).start()
    lane = lax.broadcasted_iota(jnp.int32, (128, 128), 1)
    lane2 = lax.broadcasted_iota(jnp.int32, (32, 256), 1)
    columns = jnp.where(lane == 32, mlon[:, 0:1] * wlon[:, 0:1], 0.0)
    columns = jnp.where(lane == 33, mlon[:, 255:256] * wlon[:, 255:256], columns)
    nothing = jnp.zeros((1, 256), F32)
    for k in range(16):
        row_first[k : k + 1, :] = fpad[k, 8:9, :]
        row_last[k : k + 1, :] = fpad[k, 135:136, :]
        columns = jnp.where(lane == k, fpad[k, 8:136, 255:256], columns)
        columns = jnp.where(lane == 16 + k, fpad[k, 8:136, 0:1], columns)
        fpad[k, 7:8, :] = nothing
        fpad[k, 136:137, :] = nothing
    edge[...] = columns.T[:40]

    def source(k, store, edges):
        if edges:
            west_edge, east_edge = pltpu.roll(halo_t[...], 128 - k, 1), pltpu.roll(halo_t[...], 111 - k, 1)
        for r in range(4):
            at, rows = 8 + 32 * r, slice(32 * r, 32 * r + 32)
            f = fpad[k, at : at + 32, :]
            we = jnp.concatenate([west_edge[rows]] * 2, axis=1) if edges else 0.0
            ee = jnp.concatenate([east_edge[rows]] * 2, axis=1) if edges else 0.0
            west = jnp.where(lane2 == 0, we, pltpu.roll(f, 1, 1))
            east = jnp.where(lane2 == 255, ee, pltpu.roll(f, 255, 1))
            up_down = fpad[k, at - 1 : at + 31, :] + fpad[k, at + 1 : at + 33, :]
            term = f + mlon[rows, :] * (west + east) + mlat[rows, :] * up_down
            store(rows, term * wlon[...])

    def sources(p, edges):
        def one(o, carry):
            def store(rows, value):
                send1[p, o, rows, :] = value

            source(2 * lax.rem(b + o, 8) + p, store, edges)
            return carry

        lax.fori_loop(1, 8, one, 0)

        def keep(rows, value):
            got1[p, b, rows, :] = value

        source(2 * b + p, keep, edges)

    sources(0, False)
    pl.semaphore_wait(barrier, 16)

    def remote(src, dst, send, recv, peer):
        return pltpu.make_async_remote_copy(
            src_ref=src, dst_ref=dst, send_sem=send, recv_sem=recv, device_id=peer, device_id_type=MESH
        )

    halos = [
        remote(edge.at[pl.ds(0, 16)], halo_w, h_s.at[0], h_r.at[0], lon_peer(1)),
        remote(edge.at[pl.ds(16, 16)], halo_e, h_s.at[1], h_r.at[1], lon_peer(7)),
        remote(row_last, halo_n, h_s.at[2], h_r.at[2], south),
        remote(row_first, halo_s, h_s.at[3], h_r.at[3], north),
    ]
    for c in halos:
        c.start()

    def to_lon(p, o):
        rows = pl.ds(0, FIRST) if p == 1 and o % 2 else pl.ds(0, 128)
        return remote(
            send1.at[p, o, rows], got1.at[p, b, rows], s1.at[p, o], r1.at[p, o], lon_peer(o)
        )

    def to_lon_late(o):
        rows = pl.ds(FIRST, 128 - FIRST)
        return remote(
            send1.at[1, o, rows], got1.at[1, b, rows], late_s.at[0, o], late_r.at[0, o], lon_peer(o)
        )

    for o in ORDER:
        to_lon(0, o).start()

    def basis_step(t, carry):
        for slot in range(4):
            i = t * 4 + slot
            basis_rows(i, slot).wait()

            def rows_split(r, c, slot=slot, i=i):
                high, lower = split(stage[slot, pl.ds(pl.multiple_of(r * 16, 16), 16), :])
                to = pl.ds(pl.multiple_of(i * 128 + r * 16, 16), 16)
                vh[to, :] = high
                vl[to, :] = lower
                return c

            lax.fori_loop(0, 8, rows_split, 0)

            @pl.when(t < 3)
            def _(i=i, slot=slot):
                basis_rows(i + 4, slot).start()

        return carry

    def at_step(g):
        return (pl.ds(g, 8, stride=STEPS), slice(None))

    ones, zeros = jnp.ones((8, 128), F32), jnp.zeros((8, 128), F32)

    def coefficients(p):
        def coef_block(cb, carry):
            for t in range(TILES):
                c = cb * TILES + t
                scale = ones
                for g in range(STEPS):
                    scale = -low[(p, c, *at_step(g))] * scale
                    pref[(p, c, *at_step(g))] = scale
                total, _, enter, _ = segments_combined(scale, zeros, True)
                gc[p, core, chip, pl.ds(c, 1), :] = total[7:8]
                q, w = ones, zeros
                for g in range(STEPS)[::-1]:
                    at = (p, c, *at_step(g))
                    pivot = pinv[at]
                    u = -(up[at] * pivot)
                    up[at] = u
                    w = pivot * (pref[at] * enter) + u * w
                    q = u * q
                    qref[at] = q
                    wref[at] = w
                total_q, total_w, eq, ew = segments_combined(q, w, False)
                gc[p, core, chip, pl.ds(16 + c, 1), :] = total_q[0:1]
                gc[p, core, chip, pl.ds(32 + c, 1), :] = total_w[0:1]
                seg_eq[p, c] = eq
                seg_ew[p, c] = ew
            return carry

        lax.fori_loop(0, 16 // TILES, coef_block, 0)

    def coef_to(p, o):
        return remote(
            gc.at[p, core, chip], gc.at[p, core, chip], c_s.at[p, o], c_r.at[p, o], lat_peer(o)
        )

    def coef_pair(p):
        return remote(gc.at[p, core], gc.at[p, core], c_s.at[p, 0], c_r.at[p, 0], partner)

    def fix_to(o):
        return remote(fix.at[lax.rem(b + o, 8)], fixes.at[b], f_s.at[o], f_r.at[o], lon_peer(o))

    for c in coefs:
        c.wait()
    coefficients(0)
    for o in range(1, 8):
        coef_to(0, o).start()

    for c in halos:
        c.wait()
    top = jnp.where(a > 0, halo_n[...], 0.0)
    bottom = jnp.where(a < 15, halo_s[...], 0.0)
    row_top, row_bottom = mlat[0:1, :] * top * wlon[...], mlat[127:128, :] * bottom * wlon[...]
    col_left, col_right = halo_w[...] * edge[32:33, :], halo_e[...] * edge[33:34, :]
    for d in range(8):
        k = 2 * d
        for i, row in enumerate((
            row_top[k : k + 1, :128], row_top[k : k + 1, 128:], row_bottom[k : k + 1, :128],
            row_bottom[k : k + 1, 128:], col_left[k : k + 1], col_right[k : k + 1],
        )):
            fix[d, i : i + 1, :] = row
        fpad[k + 1, 7:8, :] = top[k + 1 : k + 2]
        fpad[k + 1, 136:137, :] = bottom[k + 1 : k + 2]
    for o in range(1, 8):
        fix_to(o).start()
    fixes[b, 0:6, :] = fix[b, 0:6, :]
    halo_t[...] = jnp.concatenate([halo_w[...], halo_e[...], jnp.zeros((96, 128), F32)], axis=0).T
    sources(1, True)
    for o in ORDER:
        to_lon(1, o).start()
    lax.fori_loop(0, 4, basis_step, 0)
    coefficients(1)

    def first_half(p):
        for o in range(1, 8):
            to_lon(p, o).wait_recv()

        if p:
            for o in range(1, 8, 2):
                to_lon_late(o).wait_recv()
        else:
            for o in range(1, 8):
                fix_to(o).wait_recv()
            turned = [fixes[s, 4 + e : 5 + e, :] for e in range(2) for s in range(8)]
            fix_t[...] = jnp.concatenate(turned + [jnp.zeros((112, 128), F32)], axis=0).T

        def split_source(s, carry):
            for half in range(2):
                lanes = slice(half * 128, half * 128 + 128)
                value = got1[p, s, :, lanes]
                if p == 0:
                    row = lax.broadcasted_iota(jnp.int32, (128, 128), 0)
                    column = pltpu.roll(fix_t[...], (119 if half else 128) - s, 1)
                    value = value + jnp.where(lane == (127 if half else 0), column, 0.0)
                    value = value + jnp.where(row == 0, fixes[s, half : half + 1, :], 0.0)
                    value = value + jnp.where(row == 127, fixes[s, 2 + half : 3 + half, :], 0.0)
                high, lower = split(value)
                cols = pl.ds(pl.multiple_of(s * 256 + half * 128, 128), 128)
                pair[0:128, cols] = high
                pair[128:256, cols] = lower
            return carry

        lax.fori_loop(0, 8, split_source, 0)

        def transform(n, carry):
            cols = pl.ds(pl.multiple_of(n * 512, 512), 512)
            block = product(pair[...], vh[:, cols], vl[:, cols], NN)
            for t in range(4):
                body[p, n * 4 + t] = block[:, t * 128 : t * 128 + 128]
            return carry

        lax.fori_loop(0, 4, transform, 0)

        def solve_block(cb, carry):
            for t in range(TILES):
                c = cb * TILES + t
                x = zeros
                for g in range(STEPS):
                    at = (p, c, *at_step(g))
                    x = body[at] - low[at] * x
                    body[at] = x
                _, total, _, enter = segments_combined(pref[(p, c, *at_step(STEPS - 1))], x, True)
                gd[p, core, chip, pl.ds(c, 1), :] = total[7:8]
                y = zeros
                for g in range(STEPS)[::-1]:
                    at = (p, c, *at_step(g))
                    y = pinv[at] * (body[at] + pref[at] * enter) + up[at] * y
                    body[at] = y
                _, total, _, enter = segments_combined(qref[(p, c, *at_step(0))], y, False)
                gd[p, core, chip, pl.ds(16 + c, 1), :] = total[0:1]
                seg_eb[p, c] = enter
            return carry

        lax.fori_loop(0, 16 // TILES, solve_block, 0)
        for o in range(1, 8):
            data_to(p, o).start()

    def data_to(p, o):
        return remote(gd.at[p, core, chip], gd.at[p, core, chip], d_s.at[p, o], d_r.at[p, o], lat_peer(o))

    def data_pair(p):
        return remote(gd.at[p, core], gd.at[p, core], d_s.at[p, 0], d_r.at[p, 0], partner)

    def back_to(p, o, odd):
        rows = pl.ds(0, BACK_FIRST) if p == 0 and odd else pl.ds(0, 128)
        return remote(
            send2.at[p, o, rows], out_h.at[2 * b + p, rows], s2.at[p, o], r2.at[p, o], lon_peer(o)
        )

    def back_late(o):
        rows = pl.ds(BACK_FIRST, 128 - BACK_FIRST)
        return remote(
            send2.at[0, o, rows], out_h.at[2 * b, rows], late_s.at[1, o], late_r.at[1, o], lon_peer(o)
        )

    def second_half(p):
        for o in range(1, 8):
            data_to(p, o).wait_recv()
        data_pair(p).start()
        data_pair(p).wait_recv()
        entering, mine, entries = jnp.zeros((16, 128), F32), jnp.zeros((16, 128), F32), []
        for n in range(16):
            entries.append(entering)
            mine = jnp.where(a == n, entering, mine)
            entering = gc[p, n % 2, n // 2, 0:16, :] * entering + gd[p, n % 2, n // 2, 0:16, :]
        arriving, coming = jnp.zeros((16, 128), F32), jnp.zeros((16, 128), F32)
        for n in range(16)[::-1]:
            coming = jnp.where(a == n, arriving, coming)
            top = gd[p, n % 2, n // 2, 16:32, :] + gc[p, n % 2, n // 2, 32:48, :] * entries[n]
            arriving = gc[p, n % 2, n // 2, 16:32, :] * arriving + top
        for c in range(16):
            cols = slice(c * 128, c * 128 + 128)
            ent, arr = mine[c : c + 1], coming[c : c + 1]
            late = seg_eq[p, c] * arr + seg_eb[p, c] + seg_ew[p, c] * ent
            for s in range(8):
                rows = slice(s * 16, s * 16 + 16)
                value = body[p, c, rows] + wref[p, c, rows] * ent + qref[p, c, rows] * late[s : s + 1]
                high, lower = split(value)
                pair[rows, cols] = high
                pair[slice(128 + s * 16, 144 + s * 16), cols] = lower

        def grid_block(o):
            rows = pl.ds(pl.multiple_of(lax.rem(b + o, 8) * 256, 256), 256)
            send2[p, o] = product(pair[...], vh[rows, :], vl[rows, :], NT)

        def odd_block(t, carry):
            o = 2 * t + 1
            grid_block(o)
            back_to(p, o, True).start()
            return carry

        def even_block(t, carry):
            o = 2 * t
            grid_block(o)
            back_to(p, o, False).start()
            return carry

        lax.fori_loop(0, 4, odd_block, 0)
        lax.fori_loop(1, 4, even_block, 0)
        grid_block(0)
        own(p).start()

    def own(p):
        return copy(send2.at[p, 0], out_h.at[2 * b + p], l_own.at[p])

    def coef_forward(p):
        for o in range(1, 8):
            coef_to(p, o).wait_recv()
        coef_pair(p).start()
        coef_pair(p).wait_recv()

    first_half(0)
    for o in range(1, 8, 2):
        to_lon_late(o).start()
    for o in range(1, 8):
        coef_to(1, o).start()
    coef_forward(0)
    second_half(0)
    first_half(1)
    for o in range(1, 8, 2):
        back_late(o).start()
    coef_forward(1)
    second_half(1)
    for p in range(2):
        for o in range(1, 8):
            coef_to(p, o).wait_send()
            to_lon(p, o).wait_send()
            data_to(p, o).wait_send()
            back_to(p, o, o % 2).wait_send()
        coef_pair(p).wait_send()
        data_pair(p).wait_send()
        own(p).wait()
    for o in range(1, 8):
        fix_to(o).wait_send()
    for o in range(1, 8, 2):
        to_lon_late(o).wait_send()
        back_late(o).wait_send()
        back_late(o).wait_recv()
    for p in range(2):
        for o in range(1, 8):
            back_to(p, o, o % 2).wait_recv()


def per_device(forcing, metric_lon, metric_lat, lon_weights, eigen_basis, lower_mult, pivot_inverse, upper_coef):
    vmem, dma = pltpu.VMEM, pltpu.SemaphoreType.DMA
    band = (2, 16, 128, 128)
    scratch = [
        vmem((16, 144, 256), F32), vmem((128, 256), F32), vmem((128, 256), F32), vmem((1, 256), F32),
        vmem((16, 256), F32), vmem((16, 256), F32), vmem((16, 256), F32), vmem((16, 256), F32),
        vmem((40, 128), F32), vmem((16, 128), F32), vmem((16, 128), F32), vmem((128, 128), F32),
        vmem((2, 8, 128, 256), F32), vmem((2, 8, 128, 256), F32), vmem((4, 128, 2048), F32),
        vmem((2048, 2048), BF16), vmem((2048, 2048), BF16),
        vmem(band, F32), vmem(band, F32), vmem(band, F32), vmem(band, F32), vmem(band, F32), vmem(band, F32),
        vmem((256, 2048), BF16), vmem(band, F32),
        vmem((2, 16, 8, 128), F32), vmem((2, 16, 8, 128), F32), vmem((2, 16, 8, 128), F32),
        vmem((2, 2, 8, 48, 128), F32), vmem((2, 2, 8, 32, 128), F32), vmem((2, 8, 128, 256), F32),
        vmem((8, 8, 128), F32), vmem((8, 8, 128), F32), vmem((128, 128), F32),
        dma((4,)), dma((4,)), dma((3, 16)), dma((2,)), dma((4,)), dma((4,)), dma((2, 8)), dma((2, 8)),
        dma((2, 8)), dma((2, 8)), dma((2, 8)), dma((2, 8)), dma((2, 8)), dma((2, 8)),
        dma((8,)), dma((8,)), dma((2, 8)), dma((2, 8)),
    ]
    return pl.pallas_call(
        kernel,
        out_shape=jax.ShapeDtypeStruct((16, 128, 256), F32),
        in_specs=[pl.BlockSpec(memory_space=pl.ANY)] * 8,
        out_specs=pl.BlockSpec(memory_space=pl.ANY),
        scratch_shapes=scratch,
        compiler_params=pltpu.CompilerParams(collective_id=0, has_side_effects=True, vmem_limit_bytes=60 << 20),
    )(
        forcing, metric_lon, metric_lat, lon_weights.reshape(1, 256), eigen_basis,
        lower_mult, pivot_inverse, upper_coef,
    )


def solution(mesh):
    placed = (
        P(None, "lat", "lon"), P("lat", "lon"), P("lat", "lon"), P("lon"), P(),
        P("lon", "lat", None), P("lon", "lat", None), P("lon", "lat", None),
    )
    return jax.shard_map(
        per_device, mesh=mesh, in_specs=placed, out_specs=P(None, "lat", "lon"), check_vma=False
    )
```

```python
import functools

import jax
import jax.numpy as jnp
from jax import lax
from jax.experimental import pallas as pl
from jax.experimental.pallas import tpu as pltpu
from jax.sharding import PartitionSpec as P

MESH = pl.DeviceIdType.MESH
F32, BF16 = jnp.float32, jnp.bfloat16
NN = (((1,), (0,)), ((), ()))
NT = (((1,), (1,)), ((), ()))
TILES = 4
STEPS = 16
ORDER = (1, 3, 2, 4, 6, 5, 7)
FIRST, BACK_FIRST = 64, 64


def split(x):
    high = x.astype(BF16)
    return high, (x - high.astype(F32)).astype(BF16)


def product(pair, rhs_high, rhs_low, dims):
    dot = functools.partial(lax.dot_general, dimension_numbers=dims, preferred_element_type=F32)
    both = dot(pair, rhs_high)
    return both[:128] + both[128:] + dot(pair[:128], rhs_low)


def segments_combined(scale, shift, forward):
    row = lax.broadcasted_iota(jnp.int32, scale.shape, 0)

    def moved(x, by):
        return pltpu.roll(x, by if forward else 8 - by, 0)

    def inside(by):
        return row >= by if forward else row < 8 - by

    for by in (1, 2, 4):
        keep = inside(by)
        shift = jnp.where(keep, scale * moved(shift, by) + shift, shift)
        scale = jnp.where(keep, scale * moved(scale, by), scale)
    first = inside(1)
    return (
        scale,
        shift,
        jnp.where(first, moved(scale, 1), 1.0),
        jnp.where(first, moved(shift, 1), 0.0),
    )


def kernel(
    forcing_h, mlon_h, mlat_h, wlon_h, basis_h, low_h, pinv_h, up_h, out,
    fpad, mlon, mlat, wlon, row_last, row_first, halo_n, halo_s, edge, halo_w, halo_e, halo_t,
    send1, got1, stage, vh, vl, low, pinv, up, pref, qref, wref,
    pair, modal, body, seg_eq, seg_ew, seg_eb, gc, gd, send2,
    fix, fixes, fix_t,
    l_in, l_v, l_co, l_own, h_s, h_r, s1, r1, c_s, c_r, d_s, d_r, s2, r2,
    f_s, f_r, late_s, late_r, g_s, g_r,
):
    a, b = lax.axis_index("lat"), lax.axis_index("lon")
    chip, core = lax.div(a, 2), lax.rem(a, 2)
    copy = pltpu.make_async_copy

    inputs = [
        copy(forcing_h, fpad.at[:, pl.ds(8, 128), :], l_in.at[0]),
        copy(mlon_h, mlon, l_in.at[1]),
        copy(mlat_h, mlat, l_in.at[2]),
        copy(wlon_h, wlon, l_in.at[3]),
    ]
    for c in inputs:
        c.start()

    def basis_rows(i, slot):
        rows = pl.multiple_of(i * 128, 128)
        return copy(basis_h.at[pl.ds(rows, 128)], stage.at[slot], l_v.at[slot])

    coefs = [
        copy(src.at[:, :, pl.ds(c * 128, 128)], dst.at[:, c], l_co.at[i, c])
        for i, (src, dst) in enumerate(((low_h, low), (pinv_h, pinv), (up_h, up)))
        for c in range(16)
    ]

    def lon_peer(o):
        return {"lon": lax.rem(b + o, 8)}

    x_lo, z = lax.div(chip, 4), lax.rem(chip, 4)

    def lat_peer(o):
        return {"lat": (lax.rem(x_lo + o // 4, 2) * 4 + lax.rem(z + o % 4, 4)) * 2 + core}

    def lat_from(o):
        return lax.rem(x_lo + o // 4, 2) * 4 + lax.rem(z + 4 - o % 4, 4)

    def place(sector):
        return pl.multiple_of(lax.rem(sector, 2) * 1024 + lax.div(sector, 2) * 256, 256)

    partner = {"lat": chip * 2 + 1 - core}
    north, south = {"lat": lax.rem(a + 15, 16)}, {"lat": lax.rem(a + 1, 16)}

    barrier = pltpu.get_barrier_semaphore()
    for peer in [lon_peer(o) for o in range(1, 8)] + [lat_peer(o) for o in range(1, 8)] + [north, south]:
        pl.semaphore_signal(barrier, inc=1, device_id=peer, device_id_type=MESH)

    for c in inputs:
        c.wait()
    for c in coefs:
        c.start()
    for slot in range(4):
        basis_rows(slot, slot).start()
    lane = lax.broadcasted_iota(jnp.int32, (128, 128), 1)
    lane2 = lax.broadcasted_iota(jnp.int32, (32, 256), 1)
    columns = jnp.where(lane == 32, mlon[:, 0:1] * wlon[:, 0:1], 0.0)
    columns = jnp.where(lane == 33, mlon[:, 255:256] * wlon[:, 255:256], columns)
    nothing = jnp.zeros((1, 256), F32)
    for k in range(16):
        row_first[k : k + 1, :] = fpad[k, 8:9, :]
        row_last[k : k + 1, :] = fpad[k, 135:136, :]
        columns = jnp.where(lane == k, fpad[k, 8:136, 255:256], columns)
        columns = jnp.where(lane == 16 + k, fpad[k, 8:136, 0:1], columns)
        fpad[k, 7:8, :] = nothing
        fpad[k, 136:137, :] = nothing
    edge[...] = columns.T[:40]

    def source(k, store, edges):
        if edges:
            west_edge, east_edge = pltpu.roll(halo_t[...], 128 - k, 1), pltpu.roll(halo_t[...], 111 - k, 1)
        for r in range(4):
            at, rows = 8 + 32 * r, slice(32 * r, 32 * r + 32)
            f = fpad[k, at : at + 32, :]
            we = jnp.concatenate([west_edge[rows]] * 2, axis=1) if edges else 0.0
            ee = jnp.concatenate([east_edge[rows]] * 2, axis=1) if edges else 0.0
            west = jnp.where(lane2 == 0, we, pltpu.roll(f, 1, 1))
            east = jnp.where(lane2 == 255, ee, pltpu.roll(f, 255, 1))
            up_down = fpad[k, at - 1 : at + 31, :] + fpad[k, at + 1 : at + 33, :]
            term = f + mlon[rows, :] * (west + east) + mlat[rows, :] * up_down
            store(rows, term * wlon[...])

    def sources(p, edges):
        def one(o, carry):
            def store(rows, value):
                send1[p, o, rows, :] = value

            source(2 * lax.rem(b + o, 8) + p, store, edges)
            return carry

        lax.fori_loop(1, 8, one, 0)

        def keep(rows, value):
            got1[p, b, rows, :] = value

        source(2 * b + p, keep, edges)

    sources(0, False)
    pl.semaphore_wait(barrier, 16)

    def remote(src, dst, send, recv, peer):
        return pltpu.make_async_remote_copy(
            src_ref=src, dst_ref=dst, send_sem=send, recv_sem=recv, device_id=peer, device_id_type=MESH
        )

    halos = [
        remote(edge.at[pl.ds(0, 16)], halo_w, h_s.at[0], h_r.at[0], lon_peer(1)),
        remote(edge.at[pl.ds(16, 16)], halo_e, h_s.at[1], h_r.at[1], lon_peer(7)),
        remote(row_last, halo_n, h_s.at[2], h_r.at[2], south),
        remote(row_first, halo_s, h_s.at[3], h_r.at[3], north),
    ]
    for c in halos:
        c.start()

    def to_lon(p, o):
        rows = pl.ds(0, FIRST) if p == 1 and o % 2 else pl.ds(0, 128)
        return remote(
            send1.at[p, o, rows], got1.at[p, b, rows], s1.at[p, o], r1.at[p, o], lon_peer(o)
        )

    def to_lon_late(o):
        rows = pl.ds(FIRST, 128 - FIRST)
        return remote(
            send1.at[1, o, rows], got1.at[1, b, rows], late_s.at[0, o], late_r.at[0, o], lon_peer(o)
        )

    for o in ORDER[:5]:
        to_lon(0, o).start()

    def basis_step(t, carry):
        for slot in range(4):
            i = t * 4 + slot
            basis_rows(i, slot).wait()

            def rows_split(r, c, slot=slot, i=i):
                high, lower = split(stage[slot, pl.ds(pl.multiple_of(r * 16, 16), 16), :])
                base = place(lax.div(i, 2)) + lax.rem(i, 2) * 128
                to = pl.ds(pl.multiple_of(base + r * 16, 16), 16)
                vh[to, :] = high
                vl[to, :] = lower
                return c

            lax.fori_loop(0, 8, rows_split, 0)

            @pl.when(t < 3)
            def _(i=i, slot=slot):
                basis_rows(i + 4, slot).start()

        return carry

    def at_step(g):
        return (pl.ds(g, 8, stride=STEPS), slice(None))

    ones, zeros = jnp.ones((8, 128), F32), jnp.zeros((8, 128), F32)

    def coefficients(p):
        def coef_block(cb, carry):
            for t in range(TILES):
                c = cb * TILES + t
                scale = ones
                for g in range(STEPS):
                    scale = -low[(p, c, *at_step(g))] * scale
                    pref[(p, c, *at_step(g))] = scale
                total, _, enter, _ = segments_combined(scale, zeros, True)
                gc[p, core, chip, pl.ds(c, 1), :] = total[7:8]
                q, w = ones, zeros
                for g in range(STEPS)[::-1]:
                    at = (p, c, *at_step(g))
                    pivot = pinv[at]
                    u = -(up[at] * pivot)
                    up[at] = u
                    w = pivot * (pref[at] * enter) + u * w
                    q = u * q
                    qref[at] = q
                    wref[at] = w
                total_q, total_w, eq, ew = segments_combined(q, w, False)
                gc[p, core, chip, pl.ds(16 + c, 1), :] = total_q[0:1]
                gc[p, core, chip, pl.ds(32 + c, 1), :] = total_w[0:1]
                seg_eq[p, c] = eq
                seg_ew[p, c] = ew
            return carry

        lax.fori_loop(0, 16 // TILES, coef_block, 0)

    def coef_to(p, o):
        return remote(
            gc.at[p, core, chip], gc.at[p, core, chip], c_s.at[p, o], c_r.at[p, o], lat_peer(o)
        )

    def coef_on(p, o):
        other = lat_from(4)
        return remote(
            gc.at[p, core, other], gc.at[p, core, other], c_s.at[p, 4 + o], c_r.at[p, 4 + o], lat_peer(o)
        )

    def coef_pair(p):
        return remote(gc.at[p, core], gc.at[p, core], c_s.at[p, 0], c_r.at[p, 0], partner)

    def fix_to(o):
        return remote(fix.at[lax.rem(b + o, 8)], fixes.at[b], f_s.at[o], f_r.at[o], lon_peer(o))

    for c in coefs:
        c.wait()
    coefficients(0)
    for o in range(1, 5):
        coef_to(0, o).start()
    for o in ORDER[5:]:
        to_lon(0, o).start()
    lax.fori_loop(0, 4, basis_step, 0)

    for c in halos:
        c.wait()
    top = jnp.where(a > 0, halo_n[...], 0.0)
    bottom = jnp.where(a < 15, halo_s[...], 0.0)
    row_top, row_bottom = mlat[0:1, :] * top * wlon[...], mlat[127:128, :] * bottom * wlon[...]
    col_left, col_right = halo_w[...] * edge[32:33, :], halo_e[...] * edge[33:34, :]
    for d in range(8):
        k = 2 * d
        for i, row in enumerate((
            row_top[k : k + 1, :128], row_top[k : k + 1, 128:], row_bottom[k : k + 1, :128],
            row_bottom[k : k + 1, 128:], col_left[k : k + 1], col_right[k : k + 1],
        )):
            fix[d, i : i + 1, :] = row
        fpad[k + 1, 7:8, :] = top[k + 1 : k + 2]
        fpad[k + 1, 136:137, :] = bottom[k + 1 : k + 2]
    for o in range(1, 8):
        fix_to(o).start()
    fixes[b, 0:6, :] = fix[b, 0:6, :]
    halo_t[...] = jnp.concatenate([halo_w[...], halo_e[...], jnp.zeros((96, 128), F32)], axis=0).T
    sources(1, True)
    for o in ORDER:
        to_lon(1, o).start()
    coef_to(0, 4).wait_recv()
    for o in range(1, 4):
        coef_on(0, o).start()
    coefficients(1)
    for o in range(1, 5):
        coef_to(1, o).start()

    def transform(p, part):
        parity = lax.rem(b + part, 2)
        for o in range(2 - part, 8, 2):
            to_lon(p, o).wait_recv()
            if p == 0:
                fix_to(o).wait_recv()
            elif part:
                to_lon_late(o).wait_recv()
        if p == 0:
            turned = [fixes[2 * t + parity, 4 + e : 5 + e, :] for e in range(2) for t in range(4)]
            fix_t[...] = jnp.concatenate(turned + [jnp.zeros((120, 128), F32)], axis=0).T

        def split_source(t, carry):
            s = 2 * t + parity
            for half in range(2):
                value = got1[p, s, :, half * 128 : half * 128 + 128]
                if p == 0:
                    row = lax.broadcasted_iota(jnp.int32, (128, 128), 0)
                    column = pltpu.roll(fix_t[...], (123 if half else 128) - t, 1)
                    value = value + jnp.where(lane == (127 if half else 0), column, 0.0)
                    value = value + jnp.where(row == 0, fixes[s, half : half + 1, :], 0.0)
                    value = value + jnp.where(row == 127, fixes[s, 2 + half : 3 + half, :], 0.0)
                high, lower = split(value)
                cols = pl.ds(pl.multiple_of(place(s) + half * 128, 128), 128)
                pair[0:128, cols] = high
                pair[128:256, cols] = lower
            return carry

        lax.fori_loop(0, 4, split_source, 0)
        depth = pl.ds(pl.multiple_of(parity * 1024, 1024), 1024)

        def columns_of(n, carry):
            cols = pl.ds(pl.multiple_of(n * 512, 512), 512)
            block = product(pair[:, depth], vh[depth, cols], vl[depth, cols], NN)
            for t in range(4):
                tile = block[:, t * 128 : t * 128 + 128]
                body[p, n * 4 + t] = body[p, n * 4 + t] + tile if part else tile
            return carry

        lax.fori_loop(0, 4, columns_of, 0)

    def solve(p):
        for o in range(1, 4):
            coef_to(p, o).wait_recv()
            coef_on(p, o).wait_recv()
        coef_pair(p).start()

        def solve_block(cb, carry):
            for t in range(TILES):
                c = cb * TILES + t
                x = zeros
                for g in range(STEPS):
                    at = (p, c, *at_step(g))
                    x = body[at] - low[at] * x
                    body[at] = x
                _, total, _, enter = segments_combined(pref[(p, c, *at_step(STEPS - 1))], x, True)
                gd[p, core, chip, pl.ds(c, 1), :] = total[7:8]
                y = zeros
                for g in range(STEPS)[::-1]:
                    at = (p, c, *at_step(g))
                    y = pinv[at] * (body[at] + pref[at] * enter) + up[at] * y
                    body[at] = y
                _, total, _, enter = segments_combined(qref[(p, c, *at_step(0))], y, False)
                gd[p, core, chip, pl.ds(16 + c, 1), :] = total[0:1]
                seg_eb[p, c] = enter
            return carry

        lax.fori_loop(0, 16 // TILES, solve_block, 0)
        for o in range(1, 8):
            data_to(p, o).start()
        data_pair(p, 0).start()

    def data_to(p, o):
        return remote(gd.at[p, core, chip], gd.at[p, core, chip], d_s.at[p, o], d_r.at[p, o], lat_peer(o))

    def data_pair(p, o):
        slot = gd.at[p, core, lat_from(o)]
        return remote(slot, slot, g_s.at[p, o], g_r.at[p, o], partner)

    def back_to(p, o, odd):
        rows = pl.ds(0, BACK_FIRST) if p == 0 and odd else pl.ds(0, 128)
        return remote(
            send2.at[p, o, rows], out.at[2 * b + p, rows], s2.at[p, o], r2.at[p, o], lon_peer(o)
        )

    def back_late(o):
        rows = pl.ds(BACK_FIRST, 128 - BACK_FIRST)
        return remote(
            send2.at[0, o, rows], out.at[2 * b, rows], late_s.at[1, o], late_r.at[1, o], lon_peer(o)
        )

    def carries(p):
        for o in range(1, 8):
            data_to(p, o).wait_recv()
            data_pair(p, o).start()
        coef_pair(p).wait_recv()
        for o in range(8):
            data_pair(p, o).wait_recv()
        entering, mine, entries = jnp.zeros((16, 128), F32), jnp.zeros((16, 128), F32), []
        for n in range(16):
            entries.append(entering)
            mine = jnp.where(a == n, entering, mine)
            entering = gc[p, n % 2, n // 2, 0:16, :] * entering + gd[p, n % 2, n // 2, 0:16, :]
        arriving, coming = jnp.zeros((16, 128), F32), jnp.zeros((16, 128), F32)
        for n in range(16)[::-1]:
            coming = jnp.where(a == n, arriving, coming)
            top = gd[p, n % 2, n // 2, 16:32, :] + gc[p, n % 2, n // 2, 32:48, :] * entries[n]
            arriving = gc[p, n % 2, n // 2, 16:32, :] * arriving + top
        for c in range(16):
            cols = slice(c * 128, c * 128 + 128)
            ent, arr = mine[c : c + 1], coming[c : c + 1]
            late = seg_eq[p, c] * arr + seg_eb[p, c] + seg_ew[p, c] * ent
            for s in range(8):
                rows = slice(s * 16, s * 16 + 16)
                value = body[p, c, rows] + wref[p, c, rows] * ent + qref[p, c, rows] * late[s : s + 1]
                high, lower = split(value)
                modal[rows, cols] = high
                modal[slice(128 + s * 16, 144 + s * 16), cols] = lower

    def grid_block(p, o):
        rows = pl.ds(place(lax.rem(b + o, 8)), 256)
        send2[p, o] = product(modal[...], vh[rows, :], vl[rows, :], NT)

    def across(p):
        def block(t, carry):
            grid_block(p, 2 * t + 1)
            back_to(p, 2 * t + 1, True).start()
            return carry

        lax.fori_loop(0, 4, block, 0)

    def along(p):
        def block(t, carry):
            grid_block(p, 2 * t)
            back_to(p, 2 * t, False).start()
            return carry

        lax.fori_loop(1, 4, block, 0)
        grid_block(p, 0)
        own(p).start()

    def own(p):
        return copy(send2.at[p, 0], out.at[2 * b + p], l_own.at[p])

    transform(0, 0)
    transform(0, 1)
    solve(0)
    for o in range(1, 8, 2):
        to_lon_late(o).start()
    transform(1, 0)
    coef_to(1, 4).wait_recv()
    for o in range(1, 4):
        coef_on(1, o).start()
    carries(0)
    across(0)
    transform(1, 1)
    solve(1)
    for o in range(1, 8, 2):
        back_late(o).start()
    along(0)
    carries(1)
    across(1)
    along(1)
    for p in range(2):
        for o in range(1, 5):
            coef_to(p, o).wait_send()
        for o in range(1, 4):
            coef_on(p, o).wait_send()
        data_pair(p, 0).wait_send()
        for o in range(1, 8):
            data_pair(p, o).wait_send()
            to_lon(p, o).wait_send()
            data_to(p, o).wait_send()
            back_to(p, o, o % 2).wait_send()
        coef_pair(p).wait_send()
        own(p).wait()
    for o in range(1, 8):
        fix_to(o).wait_send()
    for o in range(1, 8, 2):
        to_lon_late(o).wait_send()
        back_late(o).wait_send()
        back_late(o).wait_recv()
    for p in range(2):
        for o in range(1, 8):
            back_to(p, o, o % 2).wait_recv()


def per_device(forcing, metric_lon, metric_lat, lon_weights, eigen_basis, lower_mult, pivot_inverse, upper_coef):
    vmem, dma = pltpu.VMEM, pltpu.SemaphoreType.DMA
    band = (2, 16, 128, 128)
    scratch = [
        vmem((16, 144, 256), F32), vmem((128, 256), F32), vmem((128, 256), F32), vmem((1, 256), F32),
        vmem((16, 256), F32), vmem((16, 256), F32), vmem((16, 256), F32), vmem((16, 256), F32),
        vmem((40, 128), F32), vmem((16, 128), F32), vmem((16, 128), F32), vmem((128, 128), F32),
        vmem((2, 8, 128, 256), F32), vmem((2, 8, 128, 256), F32), vmem((4, 128, 2048), F32),
        vmem((2048, 2048), BF16), vmem((2048, 2048), BF16),
        vmem(band, F32), vmem(band, F32), vmem(band, F32), vmem(band, F32), vmem(band, F32), vmem(band, F32),
        vmem((256, 2048), BF16), vmem((256, 2048), BF16), vmem(band, F32),
        vmem((2, 16, 8, 128), F32), vmem((2, 16, 8, 128), F32), vmem((2, 16, 8, 128), F32),
        vmem((2, 2, 8, 48, 128), F32), vmem((2, 2, 8, 32, 128), F32), vmem((2, 8, 128, 256), F32),
        vmem((8, 8, 128), F32), vmem((8, 8, 128), F32), vmem((128, 128), F32),
        dma((4,)), dma((4,)), dma((3, 16)), dma((2,)), dma((4,)), dma((4,)), dma((2, 8)), dma((2, 8)),
        dma((2, 8)), dma((2, 8)), dma((2, 8)), dma((2, 8)), dma((2, 8)), dma((2, 8)),
        dma((8,)), dma((8,)), dma((2, 8)), dma((2, 8)), dma((2, 8)), dma((2, 8)),
    ]
    return pl.pallas_call(
        kernel,
        out_shape=pltpu.VMEM((16, 128, 256), F32),
        in_specs=[pl.BlockSpec(memory_space=pl.ANY)] * 8,
        out_specs=pl.BlockSpec(memory_space=pltpu.VMEM),
        scratch_shapes=scratch,
        compiler_params=pltpu.CompilerParams(collective_id=0, has_side_effects=True, vmem_limit_bytes=60 << 20),
    )(
        forcing, metric_lon, metric_lat, lon_weights.reshape(1, 256), eigen_basis,
        lower_mult, pivot_inverse, upper_coef,
    )


def solution(mesh):
    placed = (
        P(None, "lat", "lon"), P("lat", "lon"), P("lat", "lon"), P("lon"), P(),
        P("lon", "lat", None), P("lon", "lat", None), P("lon", "lat", None),
    )
    return jax.shard_map(
        per_device, mesh=mesh, in_specs=placed, out_specs=P(None, "lat", "lon"), check_vma=False
    )
```

```python
import functools

import jax
import jax.numpy as jnp
from jax import lax
from jax.experimental import pallas as pl
from jax.experimental.pallas import tpu as pltpu
from jax.sharding import PartitionSpec as P

MESH = pl.DeviceIdType.MESH
F32, BF16 = jnp.float32, jnp.bfloat16
NN = (((1,), (0,)), ((), ()))
NT = (((1,), (1,)), ((), ()))
TILES = 4
STEPS = 16
ORDER = (1, 3, 2, 4, 6, 5, 7)
FIRST = 96


def split(x):
    high = x.astype(BF16)
    return high, (x - high.astype(F32)).astype(BF16)


def product(pair, rhs_high, rhs_low, dims):
    dot = functools.partial(lax.dot_general, dimension_numbers=dims, preferred_element_type=F32)
    both = dot(pair, rhs_high)
    return both[:128] + both[128:] + dot(pair[:128], rhs_low)


def segments_combined(scale, shift, forward):
    row = lax.broadcasted_iota(jnp.int32, scale.shape, 0)

    def moved(x, by):
        return pltpu.roll(x, by if forward else 8 - by, 0)

    def inside(by):
        return row >= by if forward else row < 8 - by

    for by in (1, 2, 4):
        keep = inside(by)
        shift = jnp.where(keep, scale * moved(shift, by) + shift, shift)
        scale = jnp.where(keep, scale * moved(scale, by), scale)
    first = inside(1)
    return (
        scale,
        shift,
        jnp.where(first, moved(scale, 1), 1.0),
        jnp.where(first, moved(shift, 1), 0.0),
    )


def kernel(
    forcing_h, mlon_h, mlat_h, wlon_h, basis_h, low_h, pinv_h, up_h, out,
    fpad, mlon, mlat, wlon, row_last, row_first, halo_n, halo_s, edge, halo_w, halo_e, halo_t,
    send1, got1, stage, vh, vl, low, pinv, up, pref, qref, wref,
    pair, modal, body, seg_eq, seg_ew, seg_eb, gc, gd, send2,
    fix, fixes, fix_t,
    l_in, l_v, l_co, l_own, h_s, h_r, s1, r1, c_s, c_r, d_s, d_r, s2, r2,
    f_s, f_r, late_s, late_r, g_s, g_r,
):
    a, b = lax.axis_index("lat"), lax.axis_index("lon")
    chip, core = lax.div(a, 2), lax.rem(a, 2)
    copy = pltpu.make_async_copy

    inputs = [
        copy(forcing_h, fpad.at[:, pl.ds(8, 128), :], l_in.at[0]),
        copy(mlon_h, mlon, l_in.at[1]),
        copy(mlat_h, mlat, l_in.at[2]),
        copy(wlon_h, wlon, l_in.at[3]),
    ]
    for c in inputs:
        c.start()

    def basis_rows(i, slot):
        rows = pl.multiple_of(i * 128, 128)
        return copy(basis_h.at[pl.ds(rows, 128)], stage.at[slot], l_v.at[slot])

    coefs = [
        copy(src.at[:, :, pl.ds(c * 128, 128)], dst.at[:, c], l_co.at[i, c])
        for i, (src, dst) in enumerate(((low_h, low), (pinv_h, pinv), (up_h, up)))
        for c in range(16)
    ]

    def lon_id(o):
        y = lax.div(b, 2)
        along_y = lax.rem(y + lax.div(o, 2), 4) * 2 + lax.rem(b, 2)
        across_x = lax.rem(y + 2 + 3 * lax.div(o, 2), 4) * 2 + 1 - lax.rem(b, 2)
        return jnp.where(lax.rem(o, 2) == 1, across_x, along_y)

    def lon_peer(o):
        return {"lon": lon_id(o)}

    x_lo, z = lax.div(chip, 4), lax.rem(chip, 4)

    def lat_peer(o):
        return {"lat": (lax.rem(x_lo + o // 4, 2) * 4 + lax.rem(z + o % 4, 4)) * 2 + core}

    def lat_from(o):
        return lax.rem(x_lo + o // 4, 2) * 4 + lax.rem(z + 4 - o % 4, 4)

    def place(sector):
        return pl.multiple_of(lax.rem(sector, 2) * 1024 + lax.div(sector, 2) * 256, 256)

    partner = {"lat": chip * 2 + 1 - core}
    north, south = {"lat": lax.rem(a + 15, 16)}, {"lat": lax.rem(a + 1, 16)}

    barrier = pltpu.get_barrier_semaphore()
    for peer in [lon_peer(o) for o in range(1, 8)] + [lat_peer(o) for o in range(1, 8)] + [north, south]:
        pl.semaphore_signal(barrier, inc=1, device_id=peer, device_id_type=MESH)

    for c in inputs:
        c.wait()
    for c in coefs:
        c.start()
    for slot in range(4):
        basis_rows(slot, slot).start()
    lane = lax.broadcasted_iota(jnp.int32, (128, 128), 1)
    lane2 = lax.broadcasted_iota(jnp.int32, (32, 256), 1)
    columns = jnp.where(lane == 32, mlon[:, 0:1] * wlon[:, 0:1], 0.0)
    columns = jnp.where(lane == 33, mlon[:, 255:256] * wlon[:, 255:256], columns)
    nothing = jnp.zeros((1, 256), F32)
    for k in range(16):
        row_first[k : k + 1, :] = fpad[k, 8:9, :]
        row_last[k : k + 1, :] = fpad[k, 135:136, :]
        columns = jnp.where(lane == k, fpad[k, 8:136, 255:256], columns)
        columns = jnp.where(lane == 16 + k, fpad[k, 8:136, 0:1], columns)
        fpad[k, 7:8, :] = nothing
        fpad[k, 136:137, :] = nothing
    edge[...] = columns.T[:40]

    def source(k, store, edges):
        if edges:
            west_edge, east_edge = pltpu.roll(halo_t[...], 128 - k, 1), pltpu.roll(halo_t[...], 111 - k, 1)
        for r in range(4):
            at, rows = 8 + 32 * r, slice(32 * r, 32 * r + 32)
            f = fpad[k, at : at + 32, :]
            we = jnp.concatenate([west_edge[rows]] * 2, axis=1) if edges else 0.0
            ee = jnp.concatenate([east_edge[rows]] * 2, axis=1) if edges else 0.0
            west = jnp.where(lane2 == 0, we, pltpu.roll(f, 1, 1))
            east = jnp.where(lane2 == 255, ee, pltpu.roll(f, 255, 1))
            up_down = fpad[k, at - 1 : at + 31, :] + fpad[k, at + 1 : at + 33, :]
            term = f + mlon[rows, :] * (west + east) + mlat[rows, :] * up_down
            store(rows, term * wlon[...])

    def sources(p, edges):
        def one(o, carry):
            def store(rows, value):
                send1[p, o, rows, :] = value

            source(2 * lon_id(o) + p, store, edges)
            return carry

        lax.fori_loop(1, 8, one, 0)

        def keep(rows, value):
            got1[p, b, rows, :] = value

        source(2 * b + p, keep, edges)

    sources(0, False)
    pl.semaphore_wait(barrier, 16)

    def remote(src, dst, send, recv, peer):
        return pltpu.make_async_remote_copy(
            src_ref=src, dst_ref=dst, send_sem=send, recv_sem=recv, device_id=peer, device_id_type=MESH
        )

    halos = [
        remote(edge.at[pl.ds(0, 16)], halo_w, h_s.at[0], h_r.at[0], {"lon": lax.rem(b + 1, 8)}),
        remote(edge.at[pl.ds(16, 16)], halo_e, h_s.at[1], h_r.at[1], {"lon": lax.rem(b + 7, 8)}),
        remote(row_last, halo_n, h_s.at[2], h_r.at[2], south),
        remote(row_first, halo_s, h_s.at[3], h_r.at[3], north),
    ]
    for c in halos:
        c.start()

    def to_lon(p, o):
        rows = pl.ds(0, FIRST) if p == 1 and o % 2 else pl.ds(0, 128)
        return remote(
            send1.at[p, o, rows], got1.at[p, b, rows], s1.at[p, o], r1.at[p, o], lon_peer(o)
        )

    def to_lon_late(o):
        rows = pl.ds(FIRST, 128 - FIRST)
        return remote(
            send1.at[1, o, rows], got1.at[1, b, rows], late_s.at[o], late_r.at[o], lon_peer(o)
        )

    for o in ORDER[:5]:
        to_lon(0, o).start()

    def basis_step(t, carry):
        for slot in range(4):
            i = t * 4 + slot
            basis_rows(i, slot).wait()

            def rows_split(r, c, slot=slot, i=i):
                high, lower = split(stage[slot, pl.ds(pl.multiple_of(r * 16, 16), 16), :])
                base = place(lax.div(i, 2)) + lax.rem(i, 2) * 128
                to = pl.ds(pl.multiple_of(base + r * 16, 16), 16)
                vh[to, :] = high
                vl[to, :] = lower
                return c

            lax.fori_loop(0, 8, rows_split, 0)

            @pl.when(t < 3)
            def _(i=i, slot=slot):
                basis_rows(i + 4, slot).start()

        return carry

    def at_step(g):
        return (pl.ds(g, 8, stride=STEPS), slice(None))

    ones, zeros = jnp.ones((8, 128), F32), jnp.zeros((8, 128), F32)

    def coefficients(p):
        def coef_block(cb, carry):
            for t in range(TILES):
                c = cb * TILES + t
                scale = ones
                for g in range(STEPS):
                    scale = -low[(p, c, *at_step(g))] * scale
                    pref[(p, c, *at_step(g))] = scale
                total, _, enter, _ = segments_combined(scale, zeros, True)
                gc[p, core, chip, pl.ds(c, 1), :] = total[7:8]
                q, w = ones, zeros
                for g in range(STEPS)[::-1]:
                    at = (p, c, *at_step(g))
                    pivot = pinv[at]
                    u = -(up[at] * pivot)
                    up[at] = u
                    w = pivot * (pref[at] * enter) + u * w
                    q = u * q
                    qref[at] = q
                    wref[at] = w
                total_q, total_w, eq, ew = segments_combined(q, w, False)
                gc[p, core, chip, pl.ds(16 + c, 1), :] = total_q[0:1]
                gc[p, core, chip, pl.ds(32 + c, 1), :] = total_w[0:1]
                seg_eq[p, c] = eq
                seg_ew[p, c] = ew
            return carry

        lax.fori_loop(0, 16 // TILES, coef_block, 0)

    def coef_to(p, o):
        return remote(
            gc.at[p, core, chip], gc.at[p, core, chip], c_s.at[p, o], c_r.at[p, o], lat_peer(o)
        )

    def coef_on(p, o):
        other = lat_from(4)
        return remote(
            gc.at[p, core, other], gc.at[p, core, other], c_s.at[p, 4 + o], c_r.at[p, 4 + o], lat_peer(o)
        )

    def coef_pair(p):
        return remote(gc.at[p, core], gc.at[p, core], c_s.at[p, 0], c_r.at[p, 0], partner)

    def fix_to(o):
        return remote(fix.at[lon_id(o)], fixes.at[b], f_s.at[o], f_r.at[o], lon_peer(o))

    for c in coefs:
        c.wait()
    coefficients(0)
    for o in range(1, 5):
        coef_to(0, o).start()
    for o in ORDER[5:]:
        to_lon(0, o).start()
    lax.fori_loop(0, 4, basis_step, 0)

    for c in halos:
        c.wait()
    top = jnp.where(a > 0, halo_n[...], 0.0)
    bottom = jnp.where(a < 15, halo_s[...], 0.0)
    row_top, row_bottom = mlat[0:1, :] * top * wlon[...], mlat[127:128, :] * bottom * wlon[...]
    col_left, col_right = halo_w[...] * edge[32:33, :], halo_e[...] * edge[33:34, :]
    for d in range(8):
        k = 2 * d
        for i, row in enumerate((
            row_top[k : k + 1, :128], row_top[k : k + 1, 128:], row_bottom[k : k + 1, :128],
            row_bottom[k : k + 1, 128:], col_left[k : k + 1], col_right[k : k + 1],
        )):
            fix[d, i : i + 1, :] = row
        fpad[k + 1, 7:8, :] = top[k + 1 : k + 2]
        fpad[k + 1, 136:137, :] = bottom[k + 1 : k + 2]
    for o in range(1, 8):
        fix_to(o).start()
    fixes[b, 0:6, :] = fix[b, 0:6, :]
    halo_t[...] = jnp.concatenate([halo_w[...], halo_e[...], jnp.zeros((96, 128), F32)], axis=0).T
    sources(1, True)
    for o in ORDER:
        to_lon(1, o).start()
    coef_to(0, 4).wait_recv()
    for o in range(1, 4):
        coef_on(0, o).start()
    coefficients(1)
    for o in range(1, 5):
        coef_to(1, o).start()

    def transform(p, part):
        parity = lax.rem(b + part, 2)
        for o in range(2 - part, 8, 2):
            to_lon(p, o).wait_recv()
            if p == 0:
                fix_to(o).wait_recv()
            elif part:
                to_lon_late(o).wait_recv()
        if p == 0:
            turned = [fixes[2 * t + parity, 4 + e : 5 + e, :] for e in range(2) for t in range(4)]
            fix_t[...] = jnp.concatenate(turned + [jnp.zeros((120, 128), F32)], axis=0).T

        def split_source(t, carry):
            s = 2 * t + parity
            for half in range(2):
                value = got1[p, s, :, half * 128 : half * 128 + 128]
                if p == 0:
                    row = lax.broadcasted_iota(jnp.int32, (128, 128), 0)
                    column = pltpu.roll(fix_t[...], (123 if half else 128) - t, 1)
                    value = value + jnp.where(lane == (127 if half else 0), column, 0.0)
                    value = value + jnp.where(row == 0, fixes[s, half : half + 1, :], 0.0)
                    value = value + jnp.where(row == 127, fixes[s, 2 + half : 3 + half, :], 0.0)
                high, lower = split(value)
                cols = pl.ds(pl.multiple_of(place(s) + half * 128, 128), 128)
                pair[0:128, cols] = high
                pair[128:256, cols] = lower
            return carry

        lax.fori_loop(0, 4, split_source, 0)
        depth = pl.ds(pl.multiple_of(parity * 1024, 1024), 1024)

        def columns_of(n, carry):
            cols = pl.ds(pl.multiple_of(n * 512, 512), 512)
            block = product(pair[:, depth], vh[depth, cols], vl[depth, cols], NN)
            for t in range(4):
                tile = block[:, t * 128 : t * 128 + 128]
                body[p, n * 4 + t] = body[p, n * 4 + t] + tile if part else tile
            return carry

        lax.fori_loop(0, 4, columns_of, 0)

    def solve(p):
        for o in range(1, 4):
            coef_to(p, o).wait_recv()
            coef_on(p, o).wait_recv()
        coef_pair(p).start()

        def forward_block(cb, carry):
            for t in range(TILES):
                c = cb * TILES + t
                x = zeros
                for g in range(STEPS):
                    at = (p, c, *at_step(g))
                    x = body[at] - low[at] * x
                    body[at] = x
                _, total, _, enter = segments_combined(pref[(p, c, *at_step(STEPS - 1))], x, True)
                gd[p, 0, core, chip, pl.ds(c, 1), :] = total[7:8]
                seg_eb[p, c] = enter
            return carry

        lax.fori_loop(0, 16 // TILES, forward_block, 0)
        for o in range(1, 8):
            data_to(p, 0, o).start()
        data_pair(p, 0, 0).start()

        def backward_block(cb, carry):
            for t in range(TILES):
                c = cb * TILES + t
                enter = seg_eb[p, c]
                y = zeros
                for g in range(STEPS)[::-1]:
                    at = (p, c, *at_step(g))
                    y = pinv[at] * (body[at] + pref[at] * enter) + up[at] * y
                    body[at] = y
                _, total, _, enter = segments_combined(qref[(p, c, *at_step(0))], y, False)
                gd[p, 1, core, chip, pl.ds(c, 1), :] = total[0:1]
                seg_eb[p, c] = enter
            return carry

        lax.fori_loop(0, 16 // TILES, backward_block, 0)
        for o in range(1, 8):
            data_to(p, 1, o).start()
        data_pair(p, 1, 0).start()

    def data_to(p, i, o):
        slot = gd.at[p, i, core, chip]
        return remote(slot, slot, d_s.at[p, i, o], d_r.at[p, i, o], lat_peer(o))

    def data_pair(p, i, o):
        slot = gd.at[p, i, core, lat_from(o)]
        return remote(slot, slot, g_s.at[p, i, o], g_r.at[p, i, o], partner)

    def back_to(p, o):
        return remote(
            send2.at[p, o], out.at[2 * b + p], s2.at[p, o], r2.at[p, o], lon_peer(o)
        )

    def carries(p):
        for i in range(2):
            for o in range(1, 8):
                data_to(p, i, o).wait_recv()
                data_pair(p, i, o).start()
        coef_pair(p).wait_recv()
        for i in range(2):
            for o in range(8):
                data_pair(p, i, o).wait_recv()
        entering, mine, entries = jnp.zeros((16, 128), F32), jnp.zeros((16, 128), F32), []
        for n in range(16):
            entries.append(entering)
            mine = jnp.where(a == n, entering, mine)
            entering = gc[p, n % 2, n // 2, 0:16, :] * entering + gd[p, 0, n % 2, n // 2]
        arriving, coming = jnp.zeros((16, 128), F32), jnp.zeros((16, 128), F32)
        for n in range(16)[::-1]:
            coming = jnp.where(a == n, arriving, coming)
            top = gd[p, 1, n % 2, n // 2] + gc[p, n % 2, n // 2, 32:48, :] * entries[n]
            arriving = gc[p, n % 2, n // 2, 16:32, :] * arriving + top
        for c in range(16):
            cols = slice(c * 128, c * 128 + 128)
            ent, arr = mine[c : c + 1], coming[c : c + 1]
            late = seg_eq[p, c] * arr + seg_eb[p, c] + seg_ew[p, c] * ent
            for s in range(8):
                rows = slice(s * 16, s * 16 + 16)
                value = body[p, c, rows] + wref[p, c, rows] * ent + qref[p, c, rows] * late[s : s + 1]
                high, lower = split(value)
                modal[rows, cols] = high
                modal[slice(128 + s * 16, 144 + s * 16), cols] = lower

    def grid_block(p, o):
        rows = pl.ds(place(lon_id(o)), 256)
        send2[p, o] = product(modal[...], vh[rows, :], vl[rows, :], NT)

    def across(p, first, last):
        def block(t, carry):
            grid_block(p, 2 * t + 1)
            back_to(p, 2 * t + 1).start()
            return carry

        lax.fori_loop(first, last, block, 0)

    def along(p):
        def block(t, carry):
            grid_block(p, 2 * t)
            back_to(p, 2 * t).start()
            return carry

        lax.fori_loop(1, 4, block, 0)
        grid_block(p, 0)
        own(p).start()

    def own(p):
        return copy(send2.at[p, 0], out.at[2 * b + p], l_own.at[p])

    transform(0, 0)
    transform(0, 1)
    solve(0)
    for o in range(1, 8, 2):
        to_lon_late(o).start()
    transform(1, 0)
    coef_to(1, 4).wait_recv()
    for o in range(1, 4):
        coef_on(1, o).start()
    carries(0)
    across(0, 0, 2)
    transform(1, 1)
    solve(1)
    across(0, 2, 4)
    along(0)
    carries(1)
    across(1, 0, 4)
    along(1)
    for p in range(2):
        for o in range(1, 5):
            coef_to(p, o).wait_send()
        for o in range(1, 4):
            coef_on(p, o).wait_send()
        for i in range(2):
            data_pair(p, i, 0).wait_send()
            for o in range(1, 8):
                data_pair(p, i, o).wait_send()
                data_to(p, i, o).wait_send()
        for o in range(1, 8):
            to_lon(p, o).wait_send()
            back_to(p, o).wait_send()
        coef_pair(p).wait_send()
        own(p).wait()
    for o in range(1, 8):
        fix_to(o).wait_send()
    for o in range(1, 8, 2):
        to_lon_late(o).wait_send()
    for p in range(2):
        for o in range(1, 8):
            back_to(p, o).wait_recv()


def per_device(forcing, metric_lon, metric_lat, lon_weights, eigen_basis, lower_mult, pivot_inverse, upper_coef):
    vmem, dma = pltpu.VMEM, pltpu.SemaphoreType.DMA
    band = (2, 16, 128, 128)
    scratch = [
        vmem((16, 144, 256), F32), vmem((128, 256), F32), vmem((128, 256), F32), vmem((1, 256), F32),
        vmem((16, 256), F32), vmem((16, 256), F32), vmem((16, 256), F32), vmem((16, 256), F32),
        vmem((40, 128), F32), vmem((16, 128), F32), vmem((16, 128), F32), vmem((128, 128), F32),
        vmem((2, 8, 128, 256), F32), vmem((2, 8, 128, 256), F32), vmem((4, 128, 2048), F32),
        vmem((2048, 2048), BF16), vmem((2048, 2048), BF16),
        vmem(band, F32), vmem(band, F32), vmem(band, F32), vmem(band, F32), vmem(band, F32), vmem(band, F32),
        vmem((256, 2048), BF16), vmem((256, 2048), BF16), vmem(band, F32),
        vmem((2, 16, 8, 128), F32), vmem((2, 16, 8, 128), F32), vmem((2, 16, 8, 128), F32),
        vmem((2, 2, 8, 48, 128), F32), vmem((2, 2, 2, 8, 16, 128), F32), vmem((2, 8, 128, 256), F32),
        vmem((8, 8, 128), F32), vmem((8, 8, 128), F32), vmem((128, 128), F32),
        dma((4,)), dma((4,)), dma((3, 16)), dma((2,)), dma((4,)), dma((4,)), dma((2, 8)), dma((2, 8)),
        dma((2, 8)), dma((2, 8)), dma((2, 2, 8)), dma((2, 2, 8)), dma((2, 8)), dma((2, 8)),
        dma((8,)), dma((8,)), dma((8,)), dma((8,)), dma((2, 2, 8)), dma((2, 2, 8)),
    ]
    return pl.pallas_call(
        kernel,
        out_shape=pltpu.VMEM((16, 128, 256), F32),
        in_specs=[pl.BlockSpec(memory_space=pl.ANY)] * 8,
        out_specs=pl.BlockSpec(memory_space=pltpu.VMEM),
        scratch_shapes=scratch,
        compiler_params=pltpu.CompilerParams(collective_id=0, has_side_effects=True, vmem_limit_bytes=60 << 20),
    )(
        forcing, metric_lon, metric_lat, lon_weights.reshape(1, 256), eigen_basis,
        lower_mult, pivot_inverse, upper_coef,
    )


def solution(mesh):
    placed = (
        P(None, "lat", "lon"), P("lat", "lon"), P("lat", "lon"), P("lon"), P(),
        P("lon", "lat", None), P("lon", "lat", None), P("lon", "lat", None),
    )
    return jax.shard_map(
        per_device, mesh=mesh, in_specs=placed, out_specs=P(None, "lat", "lon"), check_vma=False
    )
```

```python
import functools

import jax
import jax.numpy as jnp
from jax import lax
from jax.experimental import pallas as pl
from jax.experimental.pallas import tpu as pltpu
from jax.sharding import PartitionSpec as P

MESH = pl.DeviceIdType.MESH
F32, BF16 = jnp.float32, jnp.bfloat16
NN = (((1,), (0,)), ((), ()))
NT = (((1,), (1,)), ((), ()))
TILES = 4
STEPS = 16
ORDER = (1, 2, 4, 6, 3, 5, 7)
FIRST = 96


def split(x):
    high = x.astype(BF16)
    return high, (x - high.astype(F32)).astype(BF16)


def product(pair, rhs_high, rhs_low, dims):
    dot = functools.partial(lax.dot_general, dimension_numbers=dims, preferred_element_type=F32)
    both = dot(pair, rhs_high)
    return both[:128] + both[128:] + dot(pair[:128], rhs_low)


def segments_combined(scale, shift, forward):
    row = lax.broadcasted_iota(jnp.int32, scale.shape, 0)

    def moved(x, by):
        return pltpu.roll(x, by if forward else 8 - by, 0)

    def inside(by):
        return row >= by if forward else row < 8 - by

    for by in (1, 2, 4):
        keep = inside(by)
        shift = jnp.where(keep, scale * moved(shift, by) + shift, shift)
        scale = jnp.where(keep, scale * moved(scale, by), scale)
    first = inside(1)
    return (
        scale,
        shift,
        jnp.where(first, moved(scale, 1), 1.0),
        jnp.where(first, moved(shift, 1), 0.0),
    )


def kernel(
    forcing_h, mlon_h, mlat_h, wlon_h, basis_h, low_h, pinv_h, up_h, out,
    fpad, mlon, mlat, wlon, row_last, row_first, halo_n, halo_s, edge, halo_w, halo_e, halo_t,
    send1, got1, stage, vh, vl, low, pinv, up, pref, qref, wref,
    pair, modal, body, seg_eq, seg_ew, seg_eb, gc, gd, send2,
    fix, fixes, fix_t,
    l_in, l_v, l_co, l_own, h_s, h_r, s1, r1, c_s, c_r, d_s, d_r, s2, r2,
    f_s, f_r, late_s, late_r, g_s, g_r,
):
    a, b = lax.axis_index("lat"), lax.axis_index("lon")
    chip, core = lax.div(a, 2), lax.rem(a, 2)
    copy = pltpu.make_async_copy

    inputs = [
        copy(forcing_h, fpad.at[:, pl.ds(8, 128), :], l_in.at[0]),
        copy(mlon_h, mlon, l_in.at[1]),
        copy(mlat_h, mlat, l_in.at[2]),
        copy(wlon_h, wlon, l_in.at[3]),
    ]
    for c in inputs:
        c.start()

    def basis_rows(i, slot):
        rows = pl.multiple_of(i * 128, 128)
        return copy(basis_h.at[pl.ds(rows, 128)], stage.at[slot], l_v.at[slot])

    coefs = [
        copy(src.at[:, :, pl.ds(c * 128, 128)], dst.at[:, c], l_co.at[i, c])
        for i, (src, dst) in enumerate(((low_h, low), (pinv_h, pinv), (up_h, up)))
        for c in range(16)
    ]

    def lon_id(o):
        y = lax.div(b, 2)
        along_y = lax.rem(y + lax.div(o, 2), 4) * 2 + lax.rem(b, 2)
        across_x = lax.rem(y + 2 + 3 * lax.div(o, 2), 4) * 2 + 1 - lax.rem(b, 2)
        return jnp.where(lax.rem(o, 2) == 1, across_x, along_y)

    def lon_peer(o):
        return {"lon": lon_id(o)}

    x_lo, z = lax.div(chip, 4), lax.rem(chip, 4)

    def lat_peer(o):
        return {"lat": (lax.rem(x_lo + o // 4, 2) * 4 + lax.rem(z + o % 4, 4)) * 2 + core}

    def lat_from(o):
        return lax.rem(x_lo + o // 4, 2) * 4 + lax.rem(z + 4 - o % 4, 4)

    def place(sector):
        return pl.multiple_of(lax.rem(sector, 2) * 1024 + lax.div(sector, 2) * 256, 256)

    partner = {"lat": chip * 2 + 1 - core}
    north, south = {"lat": lax.rem(a + 15, 16)}, {"lat": lax.rem(a + 1, 16)}

    barrier = pltpu.get_barrier_semaphore()
    for peer in [lon_peer(o) for o in range(1, 8)] + [lat_peer(o) for o in range(1, 8)] + [north, south]:
        pl.semaphore_signal(barrier, inc=1, device_id=peer, device_id_type=MESH)

    for c in inputs:
        c.wait()
    for c in coefs:
        c.start()
    for slot in range(4):
        basis_rows(slot, slot).start()
    lane = lax.broadcasted_iota(jnp.int32, (128, 128), 1)
    lane2 = lax.broadcasted_iota(jnp.int32, (32, 256), 1)
    for k in range(16):
        fpad[k, 7:8, :] = jnp.zeros((1, 256), F32)
        fpad[k, 136:137, :] = jnp.zeros((1, 256), F32)

    def source(k, store, edges):
        if edges:
            west_edge, east_edge = pltpu.roll(halo_t[...], 128 - k, 1), pltpu.roll(halo_t[...], 111 - k, 1)
        for r in range(4):
            at, rows = 8 + 32 * r, slice(32 * r, 32 * r + 32)
            f = fpad[k, at : at + 32, :]
            we = jnp.concatenate([west_edge[rows]] * 2, axis=1) if edges else 0.0
            ee = jnp.concatenate([east_edge[rows]] * 2, axis=1) if edges else 0.0
            west = jnp.where(lane2 == 0, we, pltpu.roll(f, 1, 1))
            east = jnp.where(lane2 == 255, ee, pltpu.roll(f, 255, 1))
            up_down = fpad[k, at - 1 : at + 31, :] + fpad[k, at + 1 : at + 33, :]
            term = f + mlon[rows, :] * (west + east) + mlat[rows, :] * up_down
            store(rows, term * wlon[...])

    def sources(p, edges):
        def one(o, carry):
            def store(rows, value):
                send1[p, o, rows, :] = value

            source(2 * lon_id(o) + p, store, edges)
            return carry

        lax.fori_loop(1, 8, one, 0)

        def keep(rows, value):
            got1[p, b, rows, :] = value

        source(2 * b + p, keep, edges)

    sources(0, False)
    pl.semaphore_wait(barrier, 16)

    def remote(src, dst, send, recv, peer):
        return pltpu.make_async_remote_copy(
            src_ref=src, dst_ref=dst, send_sem=send, recv_sem=recv, device_id=peer, device_id_type=MESH
        )


    def to_lon(p, o):
        rows = pl.ds(0, FIRST) if p == 1 and o % 2 else pl.ds(0, 128)
        return remote(
            send1.at[p, o, rows], got1.at[p, b, rows], s1.at[p, o], r1.at[p, o], lon_peer(o)
        )

    def to_lon_late(o):
        rows = pl.ds(FIRST, 128 - FIRST)
        return remote(
            send1.at[1, o, rows], got1.at[1, b, rows], late_s.at[o], late_r.at[o], lon_peer(o)
        )

    for o in ORDER[:4]:
        to_lon(0, o).start()
    columns = jnp.where(lane == 32, mlon[:, 0:1] * wlon[:, 0:1], 0.0)
    columns = jnp.where(lane == 33, mlon[:, 255:256] * wlon[:, 255:256], columns)
    for k in range(16):
        row_first[k : k + 1, :] = fpad[k, 8:9, :]
        row_last[k : k + 1, :] = fpad[k, 135:136, :]
        columns = jnp.where(lane == k, fpad[k, 8:136, 255:256], columns)
        columns = jnp.where(lane == 16 + k, fpad[k, 8:136, 0:1], columns)
    edge[...] = columns.T[:40]
    halos = [
        remote(edge.at[pl.ds(0, 16)], halo_w, h_s.at[0], h_r.at[0], {"lon": lax.rem(b + 1, 8)}),
        remote(edge.at[pl.ds(16, 16)], halo_e, h_s.at[1], h_r.at[1], {"lon": lax.rem(b + 7, 8)}),
        remote(row_last, halo_n, h_s.at[2], h_r.at[2], south),
        remote(row_first, halo_s, h_s.at[3], h_r.at[3], north),
    ]
    for c in halos:
        c.start()
    to_lon(0, ORDER[4]).start()

    def basis_step(t, carry):
        for slot in range(4):
            i = t * 4 + slot
            basis_rows(i, slot).wait()

            def rows_split(r, c, slot=slot, i=i):
                high, lower = split(stage[slot, pl.ds(pl.multiple_of(r * 16, 16), 16), :])
                base = place(lax.div(i, 2)) + lax.rem(i, 2) * 128
                to = pl.ds(pl.multiple_of(base + r * 16, 16), 16)
                vh[to, :] = high
                vl[to, :] = lower
                return c

            lax.fori_loop(0, 8, rows_split, 0)

            @pl.when(t < 3)
            def _(i=i, slot=slot):
                basis_rows(i + 4, slot).start()

        return carry

    def at_step(g):
        return (pl.ds(g, 8, stride=STEPS), slice(None))

    ones, zeros = jnp.ones((8, 128), F32), jnp.zeros((8, 128), F32)

    def coefficients(p):
        def coef_block(cb, carry):
            for t in range(TILES):
                c = cb * TILES + t
                scale = ones
                for g in range(STEPS):
                    scale = -low[(p, c, *at_step(g))] * scale
                    pref[(p, c, *at_step(g))] = scale
                total, _, enter, _ = segments_combined(scale, zeros, True)
                gc[p, core, chip, pl.ds(c, 1), :] = total[7:8]
                q, w = ones, zeros
                for g in range(STEPS)[::-1]:
                    at = (p, c, *at_step(g))
                    pivot = pinv[at]
                    u = -(up[at] * pivot)
                    up[at] = u
                    w = pivot * (pref[at] * enter) + u * w
                    q = u * q
                    qref[at] = q
                    wref[at] = w
                total_q, total_w, eq, ew = segments_combined(q, w, False)
                gc[p, core, chip, pl.ds(16 + c, 1), :] = total_q[0:1]
                gc[p, core, chip, pl.ds(32 + c, 1), :] = total_w[0:1]
                seg_eq[p, c] = eq
                seg_ew[p, c] = ew
            return carry

        lax.fori_loop(0, 16 // TILES, coef_block, 0)

    def coef_to(p, o):
        return remote(
            gc.at[p, core, chip], gc.at[p, core, chip], c_s.at[p, o], c_r.at[p, o], lat_peer(o)
        )

    def coef_on(p, o):
        other = lat_from(4)
        return remote(
            gc.at[p, core, other], gc.at[p, core, other], c_s.at[p, 4 + o], c_r.at[p, 4 + o], lat_peer(o)
        )

    def coef_pair(p):
        return remote(gc.at[p, core], gc.at[p, core], c_s.at[p, 0], c_r.at[p, 0], partner)

    def fix_to(o):
        return remote(fix.at[lon_id(o)], fixes.at[b], f_s.at[o], f_r.at[o], lon_peer(o))

    for c in coefs:
        c.wait()
    coefficients(0)
    for o in range(1, 5):
        coef_to(0, o).start()
    for o in ORDER[5:]:
        to_lon(0, o).start()
    lax.fori_loop(0, 4, basis_step, 0)

    for c in halos:
        c.wait()
    top = jnp.where(a > 0, halo_n[...], 0.0)
    bottom = jnp.where(a < 15, halo_s[...], 0.0)
    row_top, row_bottom = mlat[0:1, :] * top * wlon[...], mlat[127:128, :] * bottom * wlon[...]
    col_left, col_right = halo_w[...] * edge[32:33, :], halo_e[...] * edge[33:34, :]
    for d in range(8):
        k = 2 * d
        for i, row in enumerate((
            row_top[k : k + 1, :128], row_top[k : k + 1, 128:], row_bottom[k : k + 1, :128],
            row_bottom[k : k + 1, 128:], col_left[k : k + 1], col_right[k : k + 1],
        )):
            fix[d, i : i + 1, :] = row
        fpad[k + 1, 7:8, :] = top[k + 1 : k + 2]
        fpad[k + 1, 136:137, :] = bottom[k + 1 : k + 2]
    for o in range(1, 8):
        fix_to(o).start()
    fixes[b, 0:6, :] = fix[b, 0:6, :]
    halo_t[...] = jnp.concatenate([halo_w[...], halo_e[...], jnp.zeros((96, 128), F32)], axis=0).T
    sources(1, True)
    for o in ORDER:
        to_lon(1, o).start()
    coef_to(0, 4).wait_recv()
    for o in range(1, 4):
        coef_on(0, o).start()
    coefficients(1)
    for o in range(1, 5):
        coef_to(1, o).start()

    def transform(p, part):
        parity = lax.rem(b + part, 2)
        for o in range(2 - part, 8, 2):
            to_lon(p, o).wait_recv()
            if p == 0:
                fix_to(o).wait_recv()
            elif part:
                to_lon_late(o).wait_recv()
        if p == 0:
            turned = [fixes[2 * t + parity, 4 + e : 5 + e, :] for e in range(2) for t in range(4)]
            fix_t[...] = jnp.concatenate(turned + [jnp.zeros((120, 128), F32)], axis=0).T

        def split_source(t, carry):
            s = 2 * t + parity
            for half in range(2):
                value = got1[p, s, :, half * 128 : half * 128 + 128]
                if p == 0:
                    row = lax.broadcasted_iota(jnp.int32, (128, 128), 0)
                    column = pltpu.roll(fix_t[...], (123 if half else 128) - t, 1)
                    value = value + jnp.where(lane == (127 if half else 0), column, 0.0)
                    value = value + jnp.where(row == 0, fixes[s, half : half + 1, :], 0.0)
                    value = value + jnp.where(row == 127, fixes[s, 2 + half : 3 + half, :], 0.0)
                high, lower = split(value)
                cols = pl.ds(pl.multiple_of(place(s) + half * 128, 128), 128)
                pair[0:128, cols] = high
                pair[128:256, cols] = lower
            return carry

        lax.fori_loop(0, 4, split_source, 0)
        depth = pl.ds(pl.multiple_of(parity * 1024, 1024), 1024)

        def columns_of(n, carry):
            cols = pl.ds(pl.multiple_of(n * 512, 512), 512)
            block = product(pair[:, depth], vh[depth, cols], vl[depth, cols], NN)
            for t in range(4):
                tile = block[:, t * 128 : t * 128 + 128]
                body[p, n * 4 + t] = body[p, n * 4 + t] + tile if part else tile
            return carry

        lax.fori_loop(0, 4, columns_of, 0)

    def solve(p):
        for o in range(1, 4):
            coef_to(p, o).wait_recv()
            coef_on(p, o).wait_recv()
        coef_pair(p).start()

        def forward_block(cb, carry):
            for t in range(TILES):
                c = cb * TILES + t
                x = zeros
                for g in range(STEPS):
                    at = (p, c, *at_step(g))
                    x = body[at] - low[at] * x
                    body[at] = x
                _, total, _, enter = segments_combined(pref[(p, c, *at_step(STEPS - 1))], x, True)
                gd[p, 0, core, chip, pl.ds(c, 1), :] = total[7:8]
                seg_eb[p, c] = enter
            return carry

        lax.fori_loop(0, 16 // TILES, forward_block, 0)
        for o in range(1, 8):
            data_to(p, 0, o).start()
        data_pair(p, 0, 0).start()

        def backward_block(cb, carry):
            for t in range(TILES):
                c = cb * TILES + t
                enter = seg_eb[p, c]
                y = zeros
                for g in range(STEPS)[::-1]:
                    at = (p, c, *at_step(g))
                    y = pinv[at] * (body[at] + pref[at] * enter) + up[at] * y
                    body[at] = y
                _, total, _, enter = segments_combined(qref[(p, c, *at_step(0))], y, False)
                gd[p, 1, core, chip, pl.ds(c, 1), :] = total[0:1]
                seg_eb[p, c] = enter
            return carry

        lax.fori_loop(0, 16 // TILES, backward_block, 0)
        for o in range(1, 8):
            data_to(p, 1, o).start()
        data_pair(p, 1, 0).start()

    def data_to(p, i, o):
        slot = gd.at[p, i, core, chip]
        return remote(slot, slot, d_s.at[p, i, o], d_r.at[p, i, o], lat_peer(o))

    def data_pair(p, i, o):
        slot = gd.at[p, i, core, lat_from(o)]
        return remote(slot, slot, g_s.at[p, i, o], g_r.at[p, i, o], partner)

    def back_to(p, o):
        return remote(
            send2.at[p, o], out.at[2 * b + p], s2.at[p, o], r2.at[p, o], lon_peer(o)
        )

    def carries(p):
        for i in range(2):
            for o in range(1, 8):
                data_to(p, i, o).wait_recv()
                data_pair(p, i, o).start()
        coef_pair(p).wait_recv()
        for i in range(2):
            for o in range(8):
                data_pair(p, i, o).wait_recv()
        entering, mine, entries = jnp.zeros((16, 128), F32), jnp.zeros((16, 128), F32), []
        for n in range(16):
            entries.append(entering)
            mine = jnp.where(a == n, entering, mine)
            entering = gc[p, n % 2, n // 2, 0:16, :] * entering + gd[p, 0, n % 2, n // 2]
        arriving, coming = jnp.zeros((16, 128), F32), jnp.zeros((16, 128), F32)
        for n in range(16)[::-1]:
            coming = jnp.where(a == n, arriving, coming)
            top = gd[p, 1, n % 2, n // 2] + gc[p, n % 2, n // 2, 32:48, :] * entries[n]
            arriving = gc[p, n % 2, n // 2, 16:32, :] * arriving + top
        for c in range(16):
            cols = slice(c * 128, c * 128 + 128)
            ent, arr = mine[c : c + 1], coming[c : c + 1]
            late = seg_eq[p, c] * arr + seg_eb[p, c] + seg_ew[p, c] * ent
            for s in range(8):
                rows = slice(s * 16, s * 16 + 16)
                value = body[p, c, rows] + wref[p, c, rows] * ent + qref[p, c, rows] * late[s : s + 1]
                high, lower = split(value)
                modal[rows, cols] = high
                modal[slice(128 + s * 16, 144 + s * 16), cols] = lower

    def grid_block(p, o):
        rows = pl.ds(place(lon_id(o)), 256)
        send2[p, o] = product(modal[...], vh[rows, :], vl[rows, :], NT)

    def across(p, first, last):
        def block(t, carry):
            grid_block(p, 2 * t + 1)
            back_to(p, 2 * t + 1).start()
            return carry

        lax.fori_loop(first, last, block, 0)

    def along(p):
        def block(t, carry):
            grid_block(p, 2 * t)
            back_to(p, 2 * t).start()
            return carry

        lax.fori_loop(1, 4, block, 0)
        grid_block(p, 0)
        own(p).start()

    def own(p):
        return copy(send2.at[p, 0], out.at[2 * b + p], l_own.at[p])

    transform(0, 0)
    transform(0, 1)
    solve(0)
    for o in range(1, 8, 2):
        to_lon_late(o).start()
    transform(1, 0)
    coef_to(1, 4).wait_recv()
    for o in range(1, 4):
        coef_on(1, o).start()
    carries(0)
    across(0, 0, 1)
    transform(1, 1)
    solve(1)
    across(0, 1, 4)
    along(0)
    carries(1)
    across(1, 0, 4)
    along(1)
    for p in range(2):
        for o in range(1, 5):
            coef_to(p, o).wait_send()
        for o in range(1, 4):
            coef_on(p, o).wait_send()
        for i in range(2):
            data_pair(p, i, 0).wait_send()
            for o in range(1, 8):
                data_pair(p, i, o).wait_send()
                data_to(p, i, o).wait_send()
        for o in range(1, 8):
            to_lon(p, o).wait_send()
            back_to(p, o).wait_send()
        coef_pair(p).wait_send()
        own(p).wait()
    for o in range(1, 8):
        fix_to(o).wait_send()
    for o in range(1, 8, 2):
        to_lon_late(o).wait_send()
    for p in range(2):
        for o in range(1, 8):
            back_to(p, o).wait_recv()


def per_device(forcing, metric_lon, metric_lat, lon_weights, eigen_basis, lower_mult, pivot_inverse, upper_coef):
    vmem, dma = pltpu.VMEM, pltpu.SemaphoreType.DMA
    band = (2, 16, 128, 128)
    scratch = [
        vmem((16, 144, 256), F32), vmem((128, 256), F32), vmem((128, 256), F32), vmem((1, 256), F32),
        vmem((16, 256), F32), vmem((16, 256), F32), vmem((16, 256), F32), vmem((16, 256), F32),
        vmem((40, 128), F32), vmem((16, 128), F32), vmem((16, 128), F32), vmem((128, 128), F32),
        vmem((2, 8, 128, 256), F32), vmem((2, 8, 128, 256), F32), vmem((4, 128, 2048), F32),
        vmem((2048, 2048), BF16), vmem((2048, 2048), BF16),
        vmem(band, F32), vmem(band, F32), vmem(band, F32), vmem(band, F32), vmem(band, F32), vmem(band, F32),
        vmem((256, 2048), BF16), vmem((256, 2048), BF16), vmem(band, F32),
        vmem((2, 16, 8, 128), F32), vmem((2, 16, 8, 128), F32), vmem((2, 16, 8, 128), F32),
        vmem((2, 2, 8, 48, 128), F32), vmem((2, 2, 2, 8, 16, 128), F32), vmem((2, 8, 128, 256), F32),
        vmem((8, 8, 128), F32), vmem((8, 8, 128), F32), vmem((128, 128), F32),
        dma((4,)), dma((4,)), dma((3, 16)), dma((2,)), dma((4,)), dma((4,)), dma((2, 8)), dma((2, 8)),
        dma((2, 8)), dma((2, 8)), dma((2, 2, 8)), dma((2, 2, 8)), dma((2, 8)), dma((2, 8)),
        dma((8,)), dma((8,)), dma((8,)), dma((8,)), dma((2, 2, 8)), dma((2, 2, 8)),
    ]
    return pl.pallas_call(
        kernel,
        out_shape=pltpu.VMEM((16, 128, 256), F32),
        in_specs=[pl.BlockSpec(memory_space=pl.ANY)] * 8,
        out_specs=pl.BlockSpec(memory_space=pltpu.VMEM),
        scratch_shapes=scratch,
        compiler_params=pltpu.CompilerParams(collective_id=0, has_side_effects=True, vmem_limit_bytes=60 << 20),
    )(
        forcing, metric_lon, metric_lat, lon_weights.reshape(1, 256), eigen_basis,
        lower_mult, pivot_inverse, upper_coef,
    )


def solution(mesh):
    placed = (
        P(None, "lat", "lon"), P("lat", "lon"), P("lat", "lon"), P("lon"), P(),
        P("lon", "lat", None), P("lon", "lat", None), P("lon", "lat", None),
    )
    return jax.shard_map(
        per_device, mesh=mesh, in_specs=placed, out_specs=P(None, "lat", "lon"), check_vma=False
    )
```
